128 devices in a mesh: shot: 8 (over x, core), beam: 16 (over z, y).
Axes of the slice: x: 4, y: 4, z: 4, core: 2. Of those that a mesh axis runs over, the one named last changes fastest.
Arguments:
- traces: bfloat16 [8, 4096, 128], P('shot', 'beam'), may hold values from -6 to 6
- send_table: int32 [8, 16, 16, 16], P('shot'), may hold values from 0 to 255
- window_slots: int32 [8, 128, 32], P('shot', 'beam'), may hold values from 0 to 255
- ray_depth: float32 [8, 4096, 32, 128], P('shot', 'beam'), may hold values from 0 to 0.25
- ray_lateral: float32 [4096, 32, 128], P('beam'), may hold values from 0 to 0.25
- ray_spread: float32 [4096, 32, 128], P('beam'), may hold values from 0.0001 to 0.004
- ray_index: int32 [128, 12], P('beam'), may hold values from 0 to 255
- foot_count: int32 [16, 8], P('beam'), may hold values from 1 to 12, 80 in all within a row
- foot_tiles: int32 [128, 12], replicated, may hold values from 0 to 511, as said below
- tile_owner: int32 [512], replicated, may hold values from 0 to 127, as said below
Outputs:
- image_tiles: float32 [512, 128, 128], P(('shot', 'beam'))
The draws below stay inside these ranges and needn't reach their ends.
Inputs may be any that keep to these rules, and one draw needn't show every extreme that they name: `send_table`: entry [s, j, g, i] is a row among the traces of shot gather s held by beam index j. `window_slots`: a slot of the block that the centre's group received, numbered source by source. `ray_index`: a row within the ray table of the centre's group. `foot_count`: the 8 counts of each group sum to 80. `foot_tiles`: entries past a centre's count hold tiles too; one centre's entries have distinct owners; within one group, entries whose tiles have the same owner name the same tile. `tile_owner`: each owner holds exactly 4 tiles.
All inputs are finite; a program needn't handle non-finite values.
Results may differ from the reference program's by a relative error of at most 0.0048.
Values may be sent and summed in bfloat16 or wider, within the bound.
A program may use at most 192 MiB of HBM per device.

```python
import math
import jax
import jax.numpy as jnp
import numpy as np
from jax import lax

FREQUENCIES = 64
DIRECTIONS = 32
WINDOW = 32
DEPTH_CELLS = 128
LATERAL_CELLS = 128
FOOT_SLOTS = 12
CENTRE_DEV = 8
TRACE_DEV = 256
RAY_ROWS = 256
TILE_DEV = 4
LIVE_DEV = 80
SHOT_GATHERS = 8
GROUPS = 16
OWNERS = 128
CENTRES = 128
TRACES_SHOT = 4096
RAY_TOTAL = 4096
IMAGE_TILES = 512
CAPACITY = 16


def footprint_tables(key):
    permuted = jax.random.permutation(jax.random.fold_in(key, 11), IMAGE_TILES).astype(jnp.int32)
    owner_of = permuted // TILE_DEV
    inverse = jnp.zeros((IMAGE_TILES,), jnp.int32).at[permuted].set(jnp.arange(IMAGE_TILES, dtype=jnp.int32))
    slot_pick = jax.random.randint(jax.random.fold_in(key, 12), (GROUPS, OWNERS), 0, TILE_DEV).astype(jnp.int32)
    last_owner = owner_of[IMAGE_TILES - 1]
    first_owner = owner_of[0]
    slot_pick = slot_pick.at[0, last_owner].set(permuted[IMAGE_TILES - 1] % TILE_DEV)
    slot_pick = slot_pick.at[1, first_owner].set(permuted[0] % TILE_DEV)
    candidate = inverse[jnp.arange(OWNERS, dtype=jnp.int32)[None, :] * TILE_DEV + slot_pick]
    scores = jax.random.randint(jax.random.fold_in(key, 13), (CENTRES, OWNERS), 0, 1 << 20).astype(jnp.int32) * OWNERS + jnp.arange(OWNERS, dtype=jnp.int32)[None, :]
    scores = scores.at[0, last_owner].set(-1)
    scores = scores.at[CENTRE_DEV, first_owner].set(-1)
    chosen = jnp.argsort(scores, axis=1, stable=True)[:, :FOOT_SLOTS]
    centre_group = jnp.arange(CENTRES, dtype=jnp.int32) // CENTRE_DEV
    tile_ids = candidate[centre_group[:, None], chosen]
    return (tile_ids.astype(jnp.int32), owner_of.astype(jnp.int32))


def draw_foot_tiles(key, part):
    return footprint_tables(key)[0]


def draw_tile_owner(key, part):
    return footprint_tables(key)[1]


def place_ends(values, stream_key, low, high):
    extent = values.shape
    spot = [jax.random.randint(jax.random.fold_in(stream_key, axis), (), 0, extent[axis]) for axis in range(len(extent))]
    values = values.at[tuple(spot)].set(low)
    longest = extent.index(max(extent))
    spot[longest] = (spot[longest] + 1) % extent[longest]
    return values.at[tuple(spot)].set(high)


def shard_levels(own_key, extent, cuts, low, high):
    loudness = 1.0
    for dim, shards_of in cuts:
        heights = jax.random.uniform(jax.random.fold_in(jax.random.fold_in(own_key, 6), dim), (shards_of,), jnp.float32, low / len(cuts), high / len(cuts))
        loudness = loudness * jnp.repeat(jnp.exp(heights), extent[dim] // shards_of).reshape((-1,) + (1,) * (len(extent) - 1 - dim))
    return loudness


def profile(count, total, most, slope):
    weights = [(1 << 20) // math.isqrt(rank ** slope) + 1 for rank in range(2, count + 1)]
    surplus, holding = total - most - (count - 1), [1] * (count - 1)
    while surplus > 0:
        movable = [i for i in range(count - 1) if holding[i] < most]
        pool, left = sum([weights[i] for i in movable]), surplus
        for i in movable:
            extra = min(most - holding[i], max(1, left * weights[i] // pool), surplus)
            holding[i] = holding[i] + extra
            surplus = surplus - extra
    return np.array([most] + holding)


def uneven_parts(stream_key, count, total, reach, skew):
    if count == 2:
        one = jax.random.randint(stream_key, (), max(1, total - reach), min(reach, total - 1) + 1)
        return jnp.stack([one, total - one])
    tallies = jnp.asarray(profile(count, total, reach, skew), jnp.int32)
    pairs = (count - 1) // 2
    source_of, sink = tallies[1:1 + 2 * pairs:2], tallies[2:2 + 2 * pairs:2]
    slack = jnp.minimum(source_of - 1, reach - sink)
    shifted = jax.random.randint(jax.random.fold_in(stream_key, 1), (pairs,), 0, 1 << 20) % (slack + 1)
    tallies = tallies.at[1:1 + 2 * pairs:2].set(source_of - shifted).at[2:2 + 2 * pairs:2].set(sink + shifted)
    return tallies[jax.random.permutation(jax.random.fold_in(stream_key, 2), count)]


def normal_values(own_key, dims, deviation, bound, shards=(), kind=jnp.bfloat16):
    loudness = shard_levels(own_key, dims, shards, -0.22, 0.18) if shards else 1.0
    result = jax.random.normal(own_key, dims, jnp.float32) * deviation * loudness
    return jnp.minimum(jnp.maximum(result, -bound), bound).astype(kind)


def setup_inputs(seed: int = 0) -> dict:
    streams_of = jax.random.split(jax.random.key(seed), 11)
    traces = normal_values(streams_of[0], (SHOT_GATHERS, TRACES_SHOT, 2 * FREQUENCIES), 1.0, 6.0, ((0, 8), (1, 16)))
    send_table = place_ends(jax.random.randint(streams_of[1], (SHOT_GATHERS, GROUPS, GROUPS, CAPACITY), 0, TRACE_DEV), jax.random.fold_in(streams_of[1], 1), 0, TRACE_DEV - 1).astype(jnp.int32)
    window_slots = place_ends(jax.random.randint(streams_of[2], (SHOT_GATHERS, CENTRES, WINDOW), 0, GROUPS * CAPACITY), jax.random.fold_in(streams_of[2], 1), 0, (GROUPS * CAPACITY) - 1).astype(jnp.int32)
    ray_depth = jnp.clip(0.25 * jax.random.uniform(streams_of[3], (SHOT_GATHERS, RAY_TOTAL, DIRECTIONS, DEPTH_CELLS), jnp.float32) ** shard_levels(streams_of[3], (SHOT_GATHERS, RAY_TOTAL, DIRECTIONS, DEPTH_CELLS), ((0, 8), (1, 16)), -0.2, 0.2), 0.0, 0.25)
    ray_lateral = jnp.clip(0.25 * jax.random.uniform(streams_of[4], (RAY_TOTAL, DIRECTIONS, LATERAL_CELLS), jnp.float32) ** shard_levels(streams_of[4], (RAY_TOTAL, DIRECTIONS, LATERAL_CELLS), ((0, 16),), -0.2, 0.2), 0.0, 0.25)
    ray_spread = jnp.clip(jnp.exp(math.log(0.004) - 3.6888795 * jax.random.uniform(streams_of[5], (RAY_TOTAL, DIRECTIONS, LATERAL_CELLS), jnp.float32) ** shard_levels(streams_of[5], (RAY_TOTAL, DIRECTIONS, LATERAL_CELLS), ((0, 16),), -0.2, 0.2)), 0.0001, 0.004)
    ray_index = place_ends(jax.random.randint(streams_of[6], (CENTRES, FOOT_SLOTS), 0, RAY_ROWS), jax.random.fold_in(streams_of[6], 1), 0, RAY_ROWS - 1).astype(jnp.int32)
    foot_count = jax.vmap(lambda own: uneven_parts(own, CENTRE_DEV, LIVE_DEV, FOOT_SLOTS, 2))(jax.random.split(streams_of[7], GROUPS)).reshape((GROUPS, CENTRE_DEV)).astype(jnp.int32)
    foot_tiles = draw_foot_tiles(jax.random.fold_in(streams_of[10], 71), 0)
    tile_owner = draw_tile_owner(jax.random.fold_in(streams_of[10], 71), 0)
    return {"traces": traces, "send_table": send_table, "window_slots": window_slots, "ray_depth": ray_depth, "ray_lateral": ray_lateral, "ray_spread": ray_spread, "ray_index": ray_index, "foot_count": foot_count, "foot_tiles": foot_tiles, "tile_owner": tile_owner}


def slant_tables():
    freq_index = jnp.arange(FREQUENCIES, dtype=jnp.float32)
    angular = 2.0 * math.pi * (4.0 + 60.0 * freq_index / FREQUENCIES)
    centred = jnp.arange(WINDOW, dtype=jnp.float32) - 0.5 * (WINDOW - 1)
    taper_weight = jnp.exp(-(centred / (0.25 * WINDOW)) ** 2) / math.sqrt(WINDOW)
    slowness = 2e-05 * (jnp.arange(DIRECTIONS, dtype=jnp.float32) - 0.5 * (DIRECTIONS - 1))
    stack_angle = angular[:, None, None] * slowness[None, :, None] * (25.0 * centred)[None, None, :]
    stack_real = (taper_weight * jnp.cos(stack_angle)).astype(jnp.bfloat16)
    stack_imag = (-taper_weight * jnp.sin(stack_angle)).astype(jnp.bfloat16)
    return (angular, stack_real, stack_imag)

def pair_factors(beam_real, beam_imag, depth_times, lateral_times, spread_rates, live_mask, angular):
    direction_count = beam_real.shape[1]
    freq_count = beam_real.shape[2]
    pair_count = depth_times.shape[0]
    weight_scale = (live_mask / math.sqrt(direction_count * freq_count))[:, None, None, None]
    depth_phase = angular[None, None, :, None] * depth_times[:, :, None, :]
    depth_cos = jnp.cos(depth_phase)
    depth_sin = jnp.sin(depth_phase)
    part_real = (beam_real[..., None] * depth_cos - beam_imag[..., None] * depth_sin) * weight_scale
    part_imag = (beam_real[..., None] * depth_sin + beam_imag[..., None] * depth_cos) * weight_scale
    depth_factor = jnp.stack([part_real, -part_imag], axis=1).astype(jnp.bfloat16)
    lateral_phase = angular[None, None, :, None] * lateral_times[:, :, None, :]
    damping = jnp.exp(-angular[None, None, :, None] * spread_rates[:, :, None, :])
    lateral_factor = jnp.stack([damping * jnp.cos(lateral_phase), damping * jnp.sin(lateral_phase)], axis=1).astype(jnp.bfloat16)
    depth_factor = depth_factor.reshape(pair_count, 2 * direction_count * freq_count, depth_times.shape[2])
    lateral_factor = lateral_factor.reshape(pair_count, 2 * direction_count * freq_count, lateral_times.shape[2])
    return (depth_factor, lateral_factor)

def reference(traces, send_table, window_slots, ray_depth, ray_lateral, ray_spread, ray_index, foot_count, foot_tiles, tile_owner):
    angular, stack_real, stack_imag = slant_tables()
    stack_real_wide = stack_real.astype(jnp.float32)
    stack_imag_wide = stack_imag.astype(jnp.float32)
    entries = CENTRE_DEV * FOOT_SLOTS
    entry_ids = jnp.arange(entries, dtype=jnp.int32)
    centre_local = entry_ids // FOOT_SLOTS
    slot_local = entry_ids % FOOT_SLOTS
    highest = lax.Precision.HIGHEST
    image_start = jnp.zeros((IMAGE_TILES, DEPTH_CELLS, LATERAL_CELLS), jnp.float32)

    def one_group(image_sum, flat_id):
        shot_id = flat_id // GROUPS
        group_id = flat_id % GROUPS
        slot_table = lax.dynamic_slice_in_dim(window_slots[shot_id], group_id * CENTRE_DEV, CENTRE_DEV, 0)
        source = slot_table // CAPACITY
        within = slot_table % CAPACITY
        local_rows = send_table[shot_id][source, group_id, within]
        trace_ids = source * TRACE_DEV + local_rows
        gathered = traces[shot_id][trace_ids]
        trace_real = gathered[..., :FREQUENCIES].astype(jnp.float32)
        trace_imag = gathered[..., FREQUENCIES:].astype(jnp.float32)
        beam_real = jnp.einsum('fpk,ckf->cpf', stack_real_wide, trace_real, precision=highest) - jnp.einsum('fpk,ckf->cpf', stack_imag_wide, trace_imag, precision=highest)
        beam_imag = jnp.einsum('fpk,ckf->cpf', stack_real_wide, trace_imag, precision=highest) + jnp.einsum('fpk,ckf->cpf', stack_imag_wide, trace_real, precision=highest)
        counts = foot_count[group_id]
        live_mask = (slot_local < counts[centre_local]).astype(jnp.float32)
        centre_rows = group_id * CENTRE_DEV + centre_local
        ray_rows = group_id * RAY_ROWS + ray_index[centre_rows, slot_local]
        tile_ids = foot_tiles[centre_rows, slot_local]
        depth_table = ray_depth[shot_id]

        def one_block(block_sum, block_id):
            chosen = lax.dynamic_slice_in_dim(entry_ids, block_id * 8, 8, 0)
            centres = centre_local[chosen]
            rows_now = ray_rows[chosen]
            depth_factor, lateral_factor = pair_factors(beam_real[centres], beam_imag[centres], depth_table[rows_now], ray_lateral[rows_now], ray_spread[rows_now], live_mask[chosen], angular)
            contribution = jnp.einsum('brz,brx->bzx', depth_factor.astype(jnp.float32), lateral_factor.astype(jnp.float32), precision=highest)
            return (block_sum.at[tile_ids[chosen]].add(contribution), None)
        image_sum, _ = lax.scan(one_block, image_sum, jnp.arange(entries // 8, dtype=jnp.int32))
        return (image_sum, None)
    image_full, _ = lax.scan(one_group, image_start, jnp.arange(SHOT_GATHERS * GROUPS, dtype=jnp.int32))
    tile_order = jnp.argsort(tile_owner, stable=True)
    return image_full[tile_order]
```

```python
import math, functools
import numpy as np
import jax, jax.numpy as jnp
from jax import lax
from jax.experimental import pallas as pl
from jax.experimental.pallas import tpu as pltpu

TWO_PI = 2*math.pi

def fit():
    import numpy.polynomial.chebyshev as ch, numpy.polynomial.polynomial as po
    x = np.cos(np.pi*(np.arange(400)+.5)/400)
    q = (x*0.5+0.5)*0.25
    a = 2*np.pi*np.sqrt(q)
    def f(y, deg):
        c = ch.Chebyshev.fit(q, y, deg, domain=[0, 0.25])
        return [float(v) for v in c.convert(kind=po.Polynomial).coef]
    return f(np.cos(a), 7), f(np.sin(a)/np.sqrt(q), 6)
CC, SC = fit()

def sincos_turns(t):
    r = t - jnp.round(t)
    q = r * r
    cs = CC[-1]
    for c in CC[-2::-1]:
        cs = cs * q + c
    sn = SC[-1]
    for c in SC[-2::-1]:
        sn = sn * q + c
    return cs, sn * r

NE, NS, NF, NP, NC = 10, 8, 64, 32, 8
W0 = 4.0; DW = 60.0/64; MID = 32

def lateral(tl_ref, sp_ref, l_scr, e):
    tl = tl_ref[e]; sp = sp_ref[e]
    lc, ls = sincos_turns(W0*tl)
    dm = jnp.exp(sp*(-TWO_PI*W0))
    lr = lc*dm; li = -(ls*dm)
    uc, us = sincos_turns(DW*tl)
    du = jnp.exp(sp*(-TWO_PI*DW))
    ur = uc*du; ui = -(us*du)
    for f in range(NF):
        l_scr[e, 0, f] = lr.astype(jnp.bfloat16)
        l_scr[e, 1, f] = li.astype(jnp.bfloat16)
        if f < NF-1:
            lr, li = lr*ur - li*ui, lr*ui + li*ur

def depth_unit(c, d_scr, i, tdt, bt):
    z = pl.ds(pl.multiple_of(i*16, 16), 16)
    seeds = []
    for h in range(2):
        td = tdt[h, z, :]
        c1, s1 = sincos_turns((W0+DW*MID)*td)
        uc, us = sincos_turns(DW*td)
        seeds.append((c1*uc + s1*us, s1*uc - c1*us, c1, s1, uc+uc))
    def emit(f, st):
        ar = ai = None
        for h in range(2):
            br = bt[c, h, pl.ds(f, 1), :]
            bi = bt[c, h, pl.ds(NF+f, 1), :]
            C, S = st[h][2], st[h][3]
            xr = br*C - bi*S
            xi = br*S + bi*C
            ar = xr if ar is None else ar + xr
            ai = xi if ai is None else ai + xi
        d_scr[0, z, f*128:f*128+128] = ar.astype(jnp.bfloat16)
        d_scr[1, z, f*128:f*128+128] = ai.astype(jnp.bfloat16)
    def step(st):
        return [(x[2], x[3], sd[4]*x[2]-x[0], sd[4]*x[3]-x[1]) for x, sd in zip(st, seeds)]
    st = [sd[:4] for sd in seeds]
    for f in range(MID, NF):
        emit(f, st)
        if f < NF-1: st = step(st)
    st = [(sd[2], sd[3], sd[0], sd[1]) for sd in seeds]
    for f in range(MID-1, -1, -1):
        emit(f, st)
        if f > 0: st = step(st)

def mm_unit(e, d_scr, i, l_scr, acc):
    k = pl.ds(pl.multiple_of(i*1024, 1024), 1024)
    o = acc[...]
    for part in range(2):
        l8 = l_scr[e, part, pl.ds(i*8, 8)]
        rhs = jnp.concatenate([l8[j] for j in range(8) for _ in range(4)], 0)
        o = o + jnp.dot(d_scr[part, :, k], rhs, preferred_element_type=jnp.float32)
    acc[...] = o

def main_kernel(cen_ref, td_ref, tl_ref, sp_ref, b_ref, out_ref, tdt, bt, d0, d1, l_scr, acc):
    def bprep(c, _):
        for h in range(2):
            bt[c, h] = b_ref[c, h].T
        return 0
    lax.fori_loop(0, NC, bprep, 0)
    def lprep(e, _):
        lateral(tl_ref, sp_ref, l_scr, e)
        return 0
    lax.fori_loop(0, NE, lprep, 0)
    def prep(e):
        for h in range(2):
            tdt[h] = td_ref[e, h].T
    def both(e, dst, src):
        c = cen_ref[e]
        prep(e)
        acc[...] = jnp.zeros_like(acc)
        def u(i, _):
            if src is not None:
                mm_unit(e-1, src, i, l_scr, acc)
            depth_unit(c, dst, i, tdt, bt)
            return 0
        lax.fori_loop(0, 8, u, 0)
        if src is not None:
            out_ref[e-1] = acc[...]
    both(0, d0, None)
    def pair(k, _):
        both(2*k+1, d1, d0)
        both(2*k+2, d0, d1)
        return 0
    lax.fori_loop(0, NE//2-1, pair, 0)
    both(NE-1, d1, d0)
    acc[...] = jnp.zeros_like(acc)
    def ul(i, _):
        mm_unit(NE-1, d1, i, l_scr, acc)
        return 0
    lax.fori_loop(0, 8, ul, 0)
    out_ref[NE-1] = acc[...]

def main_call(cen, td, tl, sp, b):
    vm = pl.BlockSpec(memory_space=pltpu.VMEM)
    return pl.pallas_call(
        main_kernel,
        out_shape=jax.ShapeDtypeStruct((NE, 128, 128), jnp.float32),
        in_specs=[pl.BlockSpec(memory_space=pltpu.SMEM), vm, vm, vm, vm],
        out_specs=vm,
        scratch_shapes=[pltpu.VMEM((2, 128, 128), jnp.float32), pltpu.VMEM((NC, 2, 128, 128), jnp.float32),
                        pltpu.VMEM((2, 128, NF*128), jnp.bfloat16), pltpu.VMEM((2, 128, NF*128), jnp.bfloat16), pltpu.VMEM((NE, 2, NF, 32, 128), jnp.bfloat16),
                        pltpu.VMEM((128, 128), jnp.float32)],
        name="maincore",
        compiler_params=pltpu.CompilerParams(vmem_limit_bytes=60*1024*1024),
    )(cen, td, tl, sp, b)


from jax.sharding import PartitionSpec as P

FOOT = 12
LIVE = 80


def slant_tables():
    freq_index = jnp.arange(NF, dtype=jnp.float32)
    angular = 2.0 * math.pi * (4.0 + 60.0 * freq_index / NF)
    centred = jnp.arange(32, dtype=jnp.float32) - 0.5 * 31
    taper = jnp.exp(-((centred / 8.0) ** 2)) / math.sqrt(32)
    slowness = 2e-05 * (jnp.arange(NP, dtype=jnp.float32) - 0.5 * 31)
    angle = angular[:, None, None] * slowness[None, :, None] * (25.0 * centred)[None, None, :]
    return (taper * jnp.cos(angle)).astype(jnp.bfloat16), (-taper * jnp.sin(angle)).astype(jnp.bfloat16)


def pick(index, table):
    n = table.shape[0]
    hit = index[:, None] == jnp.arange(n, dtype=jnp.int32)[None, :]
    return jnp.sum(jnp.where(hit, table[None, :], 0), axis=1)


def body(traces, send_table, window_slots, ray_depth, ray_lateral, ray_spread, ray_index, foot_count, foot_tiles, tile_owner):
    group = lax.axis_index("beam")
    shot = lax.axis_index("shot")
    incl = jnp.cumsum(foot_count[0])
    n = jnp.arange(LIVE, dtype=jnp.int32)
    cen = jnp.sum((incl[None, :] <= n[:, None]).astype(jnp.int32), axis=1)
    first = pick(cen, incl - foot_count[0])
    eid = cen * FOOT + (n - first)
    rows = pick(eid, ray_index.reshape(-1))
    tiles = pick(eid, lax.dynamic_slice_in_dim(foot_tiles, group * NC, NC, 0).reshape(-1))
    owner = pick(tiles, tile_owner)
    stack_real, stack_imag = slant_tables()
    all_rows = lax.all_gather(traces[0], "beam", axis=0, tiled=True)
    my_routes = lax.dynamic_index_in_dim(send_table[0], group, 1, keepdims=False)
    flat = (jnp.arange(16, dtype=jnp.int32)[:, None] * 256 + my_routes).reshape(-1)
    arrived = all_rows[flat]
    win = arrived[window_slots[0].reshape(-1)].reshape(NC, 32, 128)
    tr, ti = win[..., :NF], win[..., NF:]
    def es(a, b):
        return jnp.einsum("fpk,ckf->cpf", a, b, preferred_element_type=jnp.float32)
    br = es(stack_real, tr) - es(stack_imag, ti)
    bi = es(stack_real, ti) + es(stack_imag, tr)
    beam = jnp.concatenate([br, bi], axis=2) * (1.0 / math.sqrt(2048.0))
    beam_all = lax.all_gather(beam, "shot", axis=1)
    beam_all = beam_all.reshape(NC, 2, 128, 128)
    td = lax.all_to_all(ray_depth[0][rows].reshape(8, NE, 32, 128), "shot", 0, 1, tiled=False)
    td = td.reshape(NE, 2, 128, 128)
    mine = lax.dynamic_slice_in_dim(rows, shot * NE, NE, 0)
    tl = ray_lateral[mine]
    sp = ray_spread[mine]
    part = main_call(lax.dynamic_slice_in_dim(cen, shot * NE, NE, 0), td, tl, sp, beam_all)
    part = lax.all_gather(part.astype(jnp.bfloat16), "shot", axis=0, tiled=True)
    want = shot * 16 + jnp.arange(16, dtype=jnp.int32)
    sel = (owner[None, :] == want[:, None]).astype(jnp.bfloat16)
    dense = jnp.dot(sel, part.reshape(LIVE, 128 * 128), preferred_element_type=jnp.float32).astype(jnp.bfloat16)
    dense = dense.reshape(16, 128, 128)
    got = lax.all_to_all(dense, "beam", 0, 0, tiled=False).reshape(16, 128 * 128)
    me = shot * 16 + group
    same = tile_owner == me
    t = jnp.arange(512, dtype=jnp.int32)
    rank = jnp.cumsum(same.astype(jnp.int32)) - 1
    slot_of = jnp.where(same, rank, -1)
    ft = foot_tiles.reshape(16, NC * FOOT)
    slot = jnp.max(pick(ft.reshape(-1), slot_of).reshape(16, NC * FOOT), axis=1)
    place = (slot[None, :] == jnp.arange(4, dtype=jnp.int32)[:, None]).astype(jnp.bfloat16)
    out = jnp.dot(place, got, preferred_element_type=jnp.float32)
    return out.reshape(4, 128, 128)


def solution(mesh):
    in_specs = (
        P("shot", "beam", None),
        P("shot", None, None, None),
        P("shot", "beam", None),
        P("shot", "beam", None, None),
        P("beam", None, None),
        P("beam", None, None),
        P("beam", None),
        P("beam", None),
        P(),
        P(),
    )
    return jax.shard_map(body, mesh=mesh, in_specs=in_specs, out_specs=P(("shot", "beam"), None, None), check_vma=False)
```

```python
import math

import jax
import jax.numpy as jnp
import numpy as np
from jax import lax
from jax.experimental import pallas as pl
from jax.experimental.pallas import tpu as pltpu
from jax.sharding import PartitionSpec as P

MESH = pl.DeviceIdType.MESH
F32, BF16 = jnp.float32, jnp.bfloat16
NF, NP, NC, WIN, FOOT, LIVE = 64, 32, 8, 32, 12, 80
NS, NG, NE = 8, 16, 10
W0, DW, MID = 4.0, 60.0 / 64, 32
TWO_PI = 2.0 * math.pi
KP = 16
AT_ROW, AT_CEN, AT_PICK, AT_SLOT = 0, LIVE, 2 * LIVE, 2 * LIVE + NG * NC


def fit():
    x = np.cos(np.pi * (np.arange(400) + 0.5) / 400)
    q = (x * 0.5 + 0.5) * 0.25
    a = 2 * np.pi * np.sqrt(q)

    def poly(y, deg):
        c = np.polynomial.chebyshev.Chebyshev.fit(q, y, deg, domain=[0, 0.25])
        return [float(v) for v in c.convert(kind=np.polynomial.Polynomial).coef]

    return poly(np.cos(a), 7), poly(np.sin(a) / np.sqrt(q), 6)


COS_C, SIN_C = fit()


def sincos_turns(t):
    r = t - jnp.round(t)
    q = r * r
    cs = COS_C[-1]
    for c in COS_C[-2::-1]:
        cs = cs * q + c
    sn = SIN_C[-1]
    for c in SIN_C[-2::-1]:
        sn = sn * q + c
    return cs, sn * r


def stack_tables():
    f32 = np.float32
    angular = (2.0 * math.pi * (4.0 + 60.0 * np.arange(NF, dtype=f32) / NF)).astype(f32)
    centred = np.arange(WIN, dtype=f32) - f32(0.5 * (WIN - 1))
    taper = (np.exp(-((centred / f32(8.0)) ** 2)) / f32(math.sqrt(WIN))).astype(f32)
    slow = (f32(2e-05) * (np.arange(NP, dtype=f32) - f32(15.5))).astype(f32)
    angle = (angular[None, None, :] * slow[None, :, None]) * (f32(25.0) * centred)[:, None, None]
    sr = (taper[:, None, None] * np.cos(angle)).astype(BF16)
    si = (-taper[:, None, None] * np.sin(angle)).astype(BF16)
    return np.concatenate([sr, sr], 2), np.concatenate([-si, si], 2)


def lateral(tl, sp, l_scr, e):
    lc, ls = sincos_turns(W0 * tl)
    dm = jnp.exp(sp * (-TWO_PI * W0))
    lr, li = lc * dm, -(ls * dm)
    uc, us = sincos_turns(DW * tl)
    du = jnp.exp(sp * (-TWO_PI * DW))
    ur, ui = uc * du, -(us * du)
    for f in range(NF):
        l_scr[e, 0, f] = lr.astype(BF16)
        l_scr[e, 1, f] = li.astype(BF16)
        if f < NF - 1:
            lr, li = lr * ur - li * ui, lr * ui + li * ur


def depth_unit(c, d_scr, i, tdt, bt):
    z = pl.ds(pl.multiple_of(i * 16, 16), 16)
    seeds = []
    for h in range(2):
        t = tdt[h, z, :]
        c1, s1 = sincos_turns((W0 + DW * MID) * t)
        uc, us = sincos_turns(DW * t)
        seeds.append((c1 * uc + s1 * us, s1 * uc - c1 * us, c1, s1, uc + uc))

    def emit(f, st):
        ar = ai = None
        for h in range(2):
            br = bt[c, h, f : f + 1, :]
            bi = bt[c, h, NF + f : NF + f + 1, :]
            cv, sv = st[h][2], st[h][3]
            xr = br * cv - bi * sv
            xi = br * sv + bi * cv
            ar = xr if ar is None else ar + xr
            ai = xi if ai is None else ai + xi
        d_scr[f, 0, z, :] = ar.astype(BF16)
        d_scr[f, 1, z, :] = ai.astype(BF16)

    def step(st):
        return [(x[2], x[3], s[4] * x[2] - x[0], s[4] * x[3] - x[1]) for x, s in zip(st, seeds)]

    st = [s[:4] for s in seeds]
    for f in range(MID, NF):
        emit(f, st)
        if f < NF - 1:
            st = step(st)
    st = [(s[2], s[3], s[0], s[1]) for s in seeds]
    for f in range(MID - 1, -1, -1):
        emit(f, st)
        if f > 0:
            st = step(st)


def mm_piece(e, d_scr, i, l_scr, acc):
    part = i % 2
    f0 = (i // 2) * KP
    l8 = l_scr[e, part, pl.ds(f0, KP)]
    rhs = jnp.concatenate([l8[j] for j in range(KP) for _ in range(4)], 0)
    lhs = jnp.concatenate([d_scr[f0 + j, part] for j in range(KP)], 1)
    acc[...] += jnp.dot(lhs, rhs, preferred_element_type=F32)


def kernel(
    tab, traces, send_col, win_col, t0, t1, depth_hbm, lat_hbm, spr_hbm, out_ref,
    depth_v, lat_v, spr_v, tr_out, tr_in, win_s, win_r, ball, bt, td_out, td_in, tdt,
    d0, d1, l_scr, acc, tiles, dense, got,
    tab_sem, loc_sem, trs, trr, bs, br_sem, tds, tdr, tls, tlr, ds_, dr,
):
    shot = lax.axis_index("shot")
    beam = lax.axis_index("beam")
    partner = shot + 1 - 2 * lax.rem(shot, 2)

    def at_shot(s):
        return dict(device_id={"shot": s, "beam": beam}, device_id_type=MESH)

    def at_beam(g):
        return dict(device_id={"shot": shot, "beam": g}, device_id_type=MESH)

    loads = [
        pltpu.make_async_copy(h, v, tab_sem.at[n])
        for n, (h, v) in enumerate(((depth_hbm, depth_v), (lat_hbm, lat_v), (spr_hbm, spr_v)))
    ]
    for cp in loads:
        cp.start()
    barrier = pltpu.get_barrier_semaphore()
    for d in range(1, NS):
        pl.semaphore_signal(barrier, inc=1, **at_shot(lax.rem(shot + d, NS)))
    for d in range(1, NG):
        pl.semaphore_signal(barrier, inc=1, **at_beam(lax.rem(beam + d, NG)))

    lanes = lax.broadcasted_iota(jnp.int32, (256, 256), 1)
    pick = jnp.where(lanes == send_col[...], 1.0, 0.0).astype(BF16)
    chosen = jnp.dot(pick, traces[...], preferred_element_type=F32).astype(BF16)
    tr_out[...] = chosen.reshape(NG, 16, 128)
    tr_in[beam] = tr_out[beam]

    loads[0].wait()

    def gather(e, _):
        for j in range(NS):
            td_out[j, e] = depth_v[tab[AT_ROW + j * NE + e]]
        return 0

    lax.fori_loop(0, NE, gather, 0)

    def own(e, _):
        td_in[e, shot] = td_out[shot, e]
        return 0

    lax.fori_loop(0, NE, own, 0)

    pl.semaphore_wait(barrier, NS - 1 + NG - 1)

    def trace_copy(d):
        g = lax.rem(beam + d, NG)
        return pltpu.make_async_remote_copy(
            src_ref=tr_out.at[g], dst_ref=tr_in.at[beam], send_sem=trs.at[d], recv_sem=trr.at[d], **at_beam(g)
        )

    def depth_copy(e, d):
        j = lax.rem(shot + d, NS)
        return pltpu.make_async_remote_copy(
            src_ref=td_out.at[j, e], dst_ref=td_in.at[e, shot], send_sem=tds.at[e, d], recv_sem=tdr.at[e, d], **at_shot(j)
        )

    for d in range(1, NG):
        trace_copy(d).start()
    for d in range(1, NS):
        depth_copy(0, d).start()

    loads[1].wait()
    loads[2].wait()

    def lat(e, _):
        r = tab[AT_ROW + shot * NE + e]
        lateral(lat_v[r], spr_v[r], l_scr, e)
        return 0

    lax.fori_loop(0, NE // 2, lat, 0)

    for d in range(1, NG):
        trace_copy(d).wait_recv()
    pick = jnp.where(lanes == win_col[...], 1.0, 0.0).astype(BF16)
    win = jnp.dot(pick, tr_in[...].reshape(256, 128), preferred_element_type=F32)
    win_s[...] = win.reshape(NC, WIN, 128)
    win_r[...] = pltpu.roll(win, 64, 1).reshape(NC, WIN, 128)

    def stack(c, _):
        a = jnp.zeros((NP, 128), F32)
        for k in range(WIN):
            a = a + (t0[k].astype(F32) * win_s[c, k : k + 1, :] + t1[k].astype(F32) * win_r[c, k : k + 1, :])
        ball[shot, c] = a * (1.0 / math.sqrt(NP * NF))
        return 0

    lax.fori_loop(0, NC, stack, 0)

    def beam_copy(slot, n, to):
        return pltpu.make_async_remote_copy(
            src_ref=ball.at[slot], dst_ref=ball.at[slot], send_sem=bs.at[n], recv_sem=br_sem.at[n], **at_shot(to)
        )

    sends = [beam_copy(shot, d, lax.rem(shot + 2 * d, NS)) for d in range(1, 4)]
    sends.append(beam_copy(shot, 0, partner))
    for cp in sends:
        cp.start()

    def rest(e, _):
        for d in range(1, NS):
            depth_copy(e, d).start()
        return 0

    lax.fori_loop(1, NE, rest, 0)
    lax.fori_loop(NE // 2, NE, lat, 0)
    for d in range(1, 4):
        sends[d - 1].wait_recv()
        cp = beam_copy(lax.rem(shot + NS - 2 * d, NS), 3 + d, partner)
        cp.start()
        sends.append(cp)
    for cp in sends[3:]:
        cp.wait_recv()

    def turn(c, _):
        for h in range(2):
            bt[c, h] = jnp.concatenate([ball[4 * h + s, c] for s in range(4)], 0).T
        return 0

    lax.fori_loop(0, NC, turn, 0)

    def tile_copy(e, d):
        n = shot * NE + e
        return pltpu.make_async_remote_copy(
            src_ref=tiles.at[n], dst_ref=tiles.at[n], send_sem=tls.at[e, d], recv_sem=tlr.at[e, d],
            **at_shot(lax.rem(shot + d, NS)),
        )

    def share(e):
        tiles[shot * NE + e] = acc[...].astype(BF16)
        for d in range(1, NS):
            tile_copy(e, d).start()

    def both(e, dst, src):
        c = tab[AT_CEN + shot * NE + e]
        for d in range(1, NS):
            depth_copy(e, d).wait_recv()
        for h in range(2):
            tdt[h] = td_in[e, 4 * h : 4 * h + 4].reshape(128, 128).T
        acc[...] = jnp.zeros_like(acc)

        def unit(i, _):
            if src is not None:
                mm_piece(e - 1, src, i, l_scr, acc)
            depth_unit(c, dst, i, tdt, bt)
            return 0

        lax.fori_loop(0, 8, unit, 0)
        if src is not None:
            share(e - 1)

    both(0, d0, None)

    def pair(k, _):
        both(2 * k + 1, d1, d0)
        both(2 * k + 2, d0, d1)
        return 0

    lax.fori_loop(0, NE // 2 - 1, pair, 0)
    both(NE - 1, d1, d0)
    acc[...] = jnp.zeros_like(acc)

    def last(i, _):
        mm_piece(NE - 1, d1, i, l_scr, acc)
        return 0

    lax.fori_loop(0, 8, last, 0)
    share(NE - 1)
    tiles[LIVE] = jnp.zeros((128, 128), BF16)

    def arrive(e, _):
        for d in range(1, NS):
            tile_copy(e, d).wait_recv()
        return 0

    lax.fori_loop(0, NE, arrive, 0)

    def gather_owner(b, _):
        s = tiles[tab[AT_PICK + b * NC]].astype(F32)
        for m in range(1, NC):
            s = s + tiles[tab[AT_PICK + b * NC + m]].astype(F32)
        dense[b] = s.astype(BF16)
        return 0

    lax.fori_loop(0, NG, gather_owner, 0)

    def owner_copy(d):
        g = lax.rem(beam + d, NG)
        return pltpu.make_async_remote_copy(
            src_ref=dense.at[g], dst_ref=got.at[beam], send_sem=ds_.at[d], recv_sem=dr.at[d], **at_beam(g)
        )

    for d in range(1, NG):
        owner_copy(d).start()
    got[beam] = dense[beam]
    for d in range(1, NG):
        owner_copy(d).wait_recv()
    for slot in range(4):
        out_ref[slot] = jnp.zeros((128, 128), F32)

    def place(g, _):
        v = got[g].astype(F32)
        at = tab[AT_SLOT + g]
        for slot in range(4):
            out_ref[slot] += v * jnp.where(at == slot, 1.0, 0.0)
        return 0

    lax.fori_loop(0, NG, place, 0)

    for d in range(1, NG):
        trace_copy(d).wait_send()
        owner_copy(d).wait_send()
    for cp in sends:
        cp.wait_send()

    def drain(e, _):
        for d in range(1, NS):
            depth_copy(e, d).wait_send()
            tile_copy(e, d).wait_send()
        return 0

    lax.fori_loop(0, NE, drain, 0)


def fused(tab, traces, send_col, win_col, depth, lat, spr):
    t0, t1 = stack_tables()
    vm = pl.BlockSpec(memory_space=pltpu.VMEM)
    hbm = pl.BlockSpec(memory_space=pl.ANY)
    dma = pltpu.SemaphoreType.DMA
    return pl.pallas_call(
        kernel,
        out_shape=jax.ShapeDtypeStruct((4, 128, 128), F32),
        in_specs=[pl.BlockSpec(memory_space=pltpu.SMEM), vm, vm, vm, vm, vm, hbm, hbm, hbm],
        out_specs=vm,
        scratch_shapes=[
            pltpu.VMEM((256, 32, 128), F32), pltpu.VMEM((256, 32, 128), F32), pltpu.VMEM((256, 32, 128), F32),
            pltpu.VMEM((NG, 16, 128), BF16), pltpu.VMEM((NG, 16, 128), BF16),
            pltpu.VMEM((NC, WIN, 128), F32), pltpu.VMEM((NC, WIN, 128), F32),
            pltpu.VMEM((NS, NC, NP, 128), F32), pltpu.VMEM((NC, 2, 128, 128), F32),
            pltpu.VMEM((NS, NE, NP, 128), F32), pltpu.VMEM((NE, NS, NP, 128), F32), pltpu.VMEM((2, 128, 128), F32),
            pltpu.VMEM((NF, 2, 128, 128), BF16), pltpu.VMEM((NF, 2, 128, 128), BF16),
            pltpu.VMEM((NE, 2, NF, NP, 128), BF16), pltpu.VMEM((128, 128), F32),
            pltpu.VMEM((LIVE + 1, 128, 128), BF16), pltpu.VMEM((NG, 128, 128), BF16), pltpu.VMEM((NG, 128, 128), BF16),
            dma((3,)), dma((1,)), dma((NG,)), dma((NG,)), dma((7,)), dma((7,)),
            dma((NE, NS)), dma((NE, NS)), dma((NE, NS)), dma((NE, NS)), dma((NG,)), dma((NG,)),
        ],
        compiler_params=pltpu.CompilerParams(
            collective_id=0, has_side_effects=True, vmem_limit_bytes=62 * 1024 * 1024
        ),
        name="beam_migration",
    )(tab, traces, send_col, win_col, jnp.asarray(t0), jnp.asarray(t1), depth, lat, spr)


def pick_from(index, table):
    hit = index[:, None] == jnp.arange(table.shape[0], dtype=jnp.int32)[None, :]
    return jnp.sum(jnp.where(hit, table[None, :], 0), axis=1)


def scalar_table(group, shot, ray_index, foot_count, foot_tiles, tile_owner):
    i32 = jnp.int32
    counts = foot_count[0]
    lower = jnp.arange(NC)[None, :] < jnp.arange(NC)[:, None]
    before = jnp.sum(jnp.where(lower, counts[None, :], 0), axis=1)
    n = jnp.arange(LIVE, dtype=i32)
    cen = jnp.sum(((before + counts)[None, :] <= n[:, None]).astype(i32), axis=1)
    eid = cen * FOOT + n - pick_from(cen, before)
    rows = pick_from(eid, ray_index.reshape(-1))
    mine = lax.dynamic_slice_in_dim(foot_tiles, group * NC, NC, 0).reshape(-1)
    owner = pick_from(pick_from(eid, mine), tile_owner)
    same = (owner[:, None] == owner[None, :]) & (n[None, :] < n[:, None])
    rank = jnp.sum(same.astype(i32), axis=1)
    key = (owner - shot * NG) * NC + rank
    hit = key[None, :] == jnp.arange(NG * NC, dtype=i32)[:, None]
    picks = LIVE + jnp.sum(jnp.where(hit, n[None, :] - LIVE, 0), axis=1)
    me = shot * NG + group
    t = jnp.arange(512, dtype=i32)
    held = tile_owner == me
    earlier = jnp.sum((held[None, :] & (t[None, :] < t[:, None])).astype(i32), axis=1)
    slot_of = jnp.where(held, earlier, 0)
    slots = jnp.max(pick_from(foot_tiles.reshape(-1), slot_of).reshape(NG, NC * FOOT), axis=1)
    return jnp.concatenate([rows, cen, picks, slots])


def body(traces, send_table, window_slots, ray_depth, ray_lateral, ray_spread, ray_index, foot_count, foot_tiles, tile_owner):
    group = lax.axis_index("beam")
    shot = lax.axis_index("shot")
    tab = scalar_table(group, shot, ray_index, foot_count, foot_tiles, tile_owner)
    send_col = lax.dynamic_index_in_dim(send_table[0], group, 0, keepdims=False).reshape(256, 1)
    win_col = window_slots[0].reshape(256, 1)
    return fused(tab, traces[0], send_col, win_col, ray_depth[0], ray_lateral, ray_spread)


def solution(mesh):
    in_specs = (
        P("shot", "beam", None),
        P("shot", None, None, None),
        P("shot", "beam", None),
        P("shot", "beam", None, None),
        P("beam", None, None),
        P("beam", None, None),
        P("beam", None),
        P("beam", None),
        P(),
        P(),
    )
    return jax.shard_map(body, mesh=mesh, in_specs=in_specs, out_specs=P(("shot", "beam"), None, None), check_vma=False)
```

```python
import math

import jax
import jax.numpy as jnp
import numpy as np
from jax import lax
from jax.experimental import pallas as pl
from jax.experimental.pallas import tpu as pltpu
from jax.sharding import PartitionSpec as P

MESH = pl.DeviceIdType.MESH
F32, BF16 = jnp.float32, jnp.bfloat16
NF, NP, NC, WIN, FOOT, LIVE = 64, 32, 8, 32, 12, 80
NS, NG, NE = 8, 16, 10
W0, DW, MID = 4.0, 60.0 / 64, 32
TWO_PI = 2.0 * math.pi
KP = 16
EARLY = 2
AT_ROW, AT_CEN, AT_PICK, AT_SLOT = 0, 1, 2, 3


def fit():
    x = np.cos(np.pi * (np.arange(400) + 0.5) / 400)
    q = (x * 0.5 + 0.5) * 0.25
    a = 2 * np.pi * np.sqrt(q)

    def poly(y, deg):
        c = np.polynomial.chebyshev.Chebyshev.fit(q, y, deg, domain=[0, 0.25])
        return [float(v) for v in c.convert(kind=np.polynomial.Polynomial).coef]

    return poly(np.cos(a), 7), poly(np.sin(a) / np.sqrt(q), 6)


COS_C, SIN_C = fit()


def sincos_turns(t):
    r = t - jnp.round(t)
    q = r * r
    cs = COS_C[-1]
    for c in COS_C[-2::-1]:
        cs = cs * q + c
    sn = SIN_C[-1]
    for c in SIN_C[-2::-1]:
        sn = sn * q + c
    return cs, sn * r


def stack_tables():
    f32 = np.float32
    angular = (2.0 * math.pi * (4.0 + 60.0 * np.arange(NF, dtype=f32) / NF)).astype(f32)
    centred = np.arange(WIN, dtype=f32) - f32(0.5 * (WIN - 1))
    taper = (np.exp(-((centred / f32(8.0)) ** 2)) / f32(math.sqrt(WIN))).astype(f32)
    slow = (f32(2e-05) * (np.arange(NP, dtype=f32) - f32(15.5))).astype(f32)
    angle = (angular[None, None, :] * slow[None, :, None]) * (f32(25.0) * centred)[:, None, None]
    sr = (taper[:, None, None] * np.cos(angle)).astype(BF16)
    si = (-taper[:, None, None] * np.sin(angle)).astype(BF16)
    return np.concatenate([sr, sr], 2), np.concatenate([-si, si], 2)


def lateral(tl, sp, l_scr, e):
    lc, ls = sincos_turns(W0 * tl)
    dm = jnp.exp(sp * (-TWO_PI * W0))
    lr, li = lc * dm, -(ls * dm)
    uc, us = sincos_turns(DW * tl)
    du = jnp.exp(sp * (-TWO_PI * DW))
    ur, ui = uc * du, -(us * du)
    for f in range(NF):
        l_scr[e, 0, f] = lr.astype(BF16)
        l_scr[e, 1, f] = li.astype(BF16)
        if f < NF - 1:
            lr, li = lr * ur - li * ui, lr * ui + li * ur


def depth_unit(c, d_scr, i, tdt, bt):
    z = pl.ds(pl.multiple_of(i * 16, 16), 16)
    seeds = []
    for h in range(2):
        t = tdt[h, z, :]
        c1, s1 = sincos_turns((W0 + DW * MID) * t)
        uc, us = sincos_turns(DW * t)
        seeds.append((c1 * uc + s1 * us, s1 * uc - c1 * us, c1, s1, uc + uc))

    def emit(f, st):
        ar = ai = None
        for h in range(2):
            br = bt[c, h, f : f + 1, :]
            bi = bt[c, h, NF + f : NF + f + 1, :]
            cv, sv = st[h][2], st[h][3]
            xr = br * cv - bi * sv
            xi = br * sv + bi * cv
            ar = xr if ar is None else ar + xr
            ai = xi if ai is None else ai + xi
        d_scr[f, 0, z, :] = ar.astype(BF16)
        d_scr[f, 1, z, :] = ai.astype(BF16)

    def step(st):
        return [(x[2], x[3], s[4] * x[2] - x[0], s[4] * x[3] - x[1]) for x, s in zip(st, seeds)]

    st = [s[:4] for s in seeds]
    for f in range(MID, NF):
        emit(f, st)
        if f < NF - 1:
            st = step(st)
    st = [(s[2], s[3], s[0], s[1]) for s in seeds]
    for f in range(MID - 1, -1, -1):
        emit(f, st)
        if f > 0:
            st = step(st)


def mm_piece(e, d_scr, i, l_scr, acc):
    part = i % 2
    f0 = (i // 2) * KP
    l8 = l_scr[e, part, pl.ds(f0, KP)]
    rhs = jnp.concatenate([l8[j] for j in range(KP) for _ in range(4)], 0)
    lhs = jnp.concatenate([d_scr[f0 + j, part] for j in range(KP)], 1)
    acc[...] += jnp.dot(lhs, rhs, preferred_element_type=F32)


def row_to_col(row):
    return jnp.broadcast_to(row, (128, 128)).T


def prep_kernel(count, index, foot, foot_v, owner_v, out_ref):
    shot = lax.axis_index("shot")
    beam = lax.axis_index("beam")
    n = lax.broadcasted_iota(jnp.int32, (1, 128), 1)
    cen = jnp.zeros((1, 128), jnp.int32)
    base = jnp.zeros((1, 128), jnp.int32)
    total = jnp.int32(0)
    for c in range(NC):
        prior = total
        total = total + count[0, c]
        cen = cen + jnp.where(n >= total, 1, 0)
        base = jnp.where(n >= prior, prior, base)
    eid = cen * FOOT + n - base
    rows = jnp.zeros((1, 128), jnp.int32)
    tile = jnp.zeros((1, 128), jnp.int32)
    for c in range(NC):
        for k in range(FOOT):
            hit = eid == c * FOOT + k
            rows = jnp.where(hit, index[c, k], rows)
            tile = jnp.where(hit, foot[beam * NC + c, k], tile)
    live = n < LIVE
    down = lax.broadcasted_iota(jnp.int32, (128, 128), 0).astype(F32)
    across = lax.broadcasted_iota(jnp.int32, (128, 128), 1).astype(F32)
    tile = tile.astype(F32)
    owners = owner_v[...].astype(F32)
    owner = jnp.zeros((1, 128), F32)
    for q in range(OWN_ROWS):
        hit = down + 128.0 * q == tile
        owner = owner + jnp.sum(jnp.where(hit, row_to_col(owners[q : q + 1]), 0.0), axis=0, keepdims=True)
    owner = jnp.where(live, owner, -1.0)
    same = (row_to_col(owner) == owner) & (down < across)
    rank = jnp.sum(jnp.where(same, 1.0, 0.0), axis=0, keepdims=True)
    key = jnp.where(live, (owner - (shot * NG).astype(F32)) * NC + rank, -1.0)
    hit = row_to_col(key) == across
    picks = LIVE + jnp.sum(jnp.where(hit, down - LIVE, 0.0), axis=0, keepdims=True)
    me = (shot * NG + beam).astype(F32)
    number = (
        lax.broadcasted_iota(jnp.int32, (OWN_ROWS, 128), 0) * 128 + lax.broadcasted_iota(jnp.int32, (OWN_ROWS, 128), 1)
    ).astype(F32)
    held = owners == me
    named = foot_v[...].astype(F32)
    slot = jnp.zeros(named.shape, F32)
    at = jnp.full((1, 1), -1.0, F32)
    for i in range(4):
        left = jnp.where(held & (number > at), number, 1e6)
        at = jnp.min(jnp.min(left, axis=0, keepdims=True), axis=1, keepdims=True)
        slot = jnp.where(named == at, float(i), slot)
    slot = jnp.max(slot, axis=1, keepdims=True)
    slot = jnp.broadcast_to(slot, (slot.shape[0], 128))
    if slot.shape[0] < 128:
        slot = jnp.concatenate([slot, jnp.zeros((128 - slot.shape[0], 128), F32)], 0)
    slot = slot.T[0:1]
    out_ref[...] = jnp.zeros((8, 128), jnp.int32)
    out_ref[AT_ROW : AT_ROW + 1] = rows
    out_ref[AT_CEN : AT_CEN + 1] = jnp.minimum(cen, NC - 1)
    out_ref[AT_PICK : AT_PICK + 1] = picks.astype(jnp.int32)
    out_ref[AT_SLOT : AT_SLOT + 1] = slot.astype(jnp.int32)


OWN_ROWS = NS * NG * 4 // 128


def prep(foot_count, ray_index, foot_tiles, tile_owner):
    vm, sm = pl.BlockSpec(memory_space=pltpu.VMEM), pl.BlockSpec(memory_space=pltpu.SMEM)
    return pl.pallas_call(
        prep_kernel,
        out_shape=jax.ShapeDtypeStruct((8, 128), jnp.int32),
        in_specs=[sm, sm, sm, vm, vm],
        out_specs=vm,
        name="entry_table",
    )(foot_count, ray_index, foot_tiles, foot_tiles, tile_owner.reshape(OWN_ROWS, 128))


def one_hot(x, count, width):
    xt = jnp.concatenate([x.astype(F32), jnp.zeros((x.shape[0], 128 - count), F32)], 1).T
    lanes = lax.broadcasted_iota(jnp.int32, (count, width), 1).astype(F32)
    parts = [jnp.where(lanes == xt[:count, r : r + 1], 1.0, 0.0) for r in range(x.shape[0])]
    return jnp.concatenate(parts, 0).astype(BF16)


def kernel(
    tab, traces, send_ref, win_ref, t0_hbm, t1_hbm, depth_hbm, lat_hbm, spr_hbm, out_ref,
    t0, t1, depth_v, lat_v, spr_v, tr_out, tr_in, win_s, win_r, ball, b_own, b_out, b_in, bt, td_out, td_in, tdt,
    d0, d1, l_scr, acc, tiles, dense, got,
    tab_sem, trs, trr, bs, br_sem, bes, ber, tds, tdr, tls, tlr, ows, owr,
):
    shot = lax.axis_index("shot")
    beam = lax.axis_index("beam")
    partner = shot + 1 - 2 * lax.rem(shot, 2)

    def at_shot(s):
        return dict(device_id={"shot": s, "beam": beam}, device_id_type=MESH)

    def at_beam(g):
        return dict(device_id={"shot": shot, "beam": g}, device_id_type=MESH)

    barrier = pltpu.get_barrier_semaphore()
    for d in range(1, NG):
        pl.semaphore_signal(barrier, inc=1, **at_beam(lax.rem(beam + d, NG)))
    for d in range(1, NS):
        pl.semaphore_signal(barrier, inc=1, **at_shot(lax.rem(shot + d, NS)))
    pairs = ((depth_hbm, depth_v), (lat_hbm, lat_v), (spr_hbm, spr_v), (t0_hbm, t0), (t1_hbm, t1))
    loads = [pltpu.make_async_copy(h, v, tab_sem.at[n]) for n, (h, v) in enumerate(pairs)]
    for cp in loads:
        cp.start()

    pick = one_hot(send_ref[beam], 16, 256)
    chosen = jnp.dot(pick, traces[...], preferred_element_type=F32).astype(BF16)
    tr_out[...] = chosen.reshape(NG, 16, 128)
    tr_in[beam] = tr_out[beam]
    pl.semaphore_wait(barrier, NS - 1 + NG - 1)

    def trace_copy(d):
        g = lax.rem(beam + d, NG)
        return pltpu.make_async_remote_copy(
            src_ref=tr_out.at[g], dst_ref=tr_in.at[beam], send_sem=trs.at[d], recv_sem=trr.at[d], **at_beam(g)
        )

    for d in range(1, NG):
        trace_copy(d).start()

    loads[0].wait()

    def gather(e, _):
        for j in range(NS):
            td_out[j, e] = depth_v[tab[AT_ROW, j * NE + e]]
        td_in[e, shot] = depth_v[tab[AT_ROW, shot * NE + e]]
        return 0

    lax.fori_loop(0, NE, gather, 0)

    def depth_copy(e, d):
        j = lax.rem(shot + d, NS)
        return pltpu.make_async_remote_copy(
            src_ref=td_out.at[j, e], dst_ref=td_in.at[e, shot], send_sem=tds.at[e, d], recv_sem=tdr.at[e, d], **at_shot(j)
        )

    for d in range(1, NS):
        depth_copy(0, d).start()
    loads[1].wait()
    loads[2].wait()

    def lat(e, _):
        r = tab[AT_ROW, shot * NE + e]
        lateral(lat_v[r], spr_v[r], l_scr, e)
        return 0

    lax.fori_loop(0, NE // 2, lat, 0)
    pick = one_hot(win_ref[...], WIN, NG * 16)
    loads[3].wait()
    loads[4].wait()

    for d in range(1, NG):
        trace_copy(d).wait_recv()
    win = jnp.dot(pick, tr_in[...].reshape(NG * 16, 128), preferred_element_type=F32)
    win_s[...] = win.reshape(NC, WIN, 128)
    win_r[...] = pltpu.roll(win, 64, 1).reshape(NC, WIN, 128)

    def stack(c, _):
        a = jnp.zeros((NP, 128), F32)
        for k in range(WIN):
            a = a + (t0[k].astype(F32) * win_s[c, k : k + 1, :] + t1[k].astype(F32) * win_r[c, k : k + 1, :])
        b_own[c] = a * (1.0 / math.sqrt(NP * NF))
        return 0

    lax.fori_loop(0, NC, stack, 0)

    def early_copy(e, d):
        j = lax.rem(shot + d, NS)
        return pltpu.make_async_remote_copy(
            src_ref=b_out.at[j, e], dst_ref=b_in.at[e, shot], send_sem=bes.at[e, d], recv_sem=ber.at[e, d], **at_shot(j)
        )

    for e in range(EARLY):
        for j in range(NS):
            b_out[j, e] = b_own[tab[AT_CEN, j * NE + e]]
        b_in[e, shot] = b_own[tab[AT_CEN, shot * NE + e]]
        for d in range(1, NS):
            early_copy(e, d).start()
        for d in range(1, NS):
            depth_copy(e + 1, d).start()

    def beam_copy(slot, n, to, own=True):
        return pltpu.make_async_remote_copy(
            src_ref=b_own if own else ball.at[slot], dst_ref=ball.at[slot], send_sem=bs.at[n], recv_sem=br_sem.at[n], **at_shot(to)
        )

    sends = [beam_copy(shot, 0, partner)]
    sends += [beam_copy(shot, d, lax.rem(shot + 2 * d, NS)) for d in range(1, 4)]
    for cp in sends:
        cp.start()

    def rest(e, _):
        for d in range(1, NS):
            depth_copy(e, d).start()
        return 0

    lax.fori_loop(EARLY + 1, NE, rest, 0)
    ball[shot] = b_own[...]
    lax.fori_loop(NE // 2, NE, lat, 0)

    def tile_copy(e, d):
        n = shot * NE + e
        return pltpu.make_async_remote_copy(
            src_ref=tiles.at[n], dst_ref=tiles.at[n], send_sem=tls.at[e, d], recv_sem=tlr.at[e, d],
            **at_shot(lax.rem(shot + d, NS)),
        )

    def share(e):
        tiles[shot * NE + e] = acc[...].astype(BF16)
        for d in range(1, NS):
            tile_copy(e, d).start()

    def both(e, c, dst, src):
        for d in range(1, NS):
            depth_copy(e, d).wait_recv()
        for h in range(2):
            tdt[h] = td_in[e, 4 * h : 4 * h + 4].reshape(128, 128).T
        acc[...] = jnp.zeros_like(acc)

        def unit(i, _):
            if src is not None:
                mm_piece(e - 1, src, i, l_scr, acc)
            depth_unit(c, dst, i, tdt, bt)
            return 0

        lax.fori_loop(0, 8, unit, 0)
        if src is not None:
            share(e - 1)

    def early(e):
        for d in range(1, NS):
            early_copy(e, d).wait_recv()
        for h in range(2):
            bt[NC + e, h] = b_in[e, 4 * h : 4 * h + 4].reshape(128, 128).T

    early(0)
    both(0, NC, d0, None)
    for d in range(1, 4):
        sends[d].wait_recv()
        cp = beam_copy(lax.rem(shot + NS - 2 * d, NS), 3 + d, partner, False)
        cp.start()
        sends.append(cp)
    early(1)
    both(1, NC + 1, d1, d0)
    for cp in sends[:1] + sends[4:]:
        cp.wait_recv()

    def turn(c, _):
        for h in range(2):
            bt[c, h] = jnp.concatenate([ball[4 * h + s, c] for s in range(4)], 0).T
        return 0

    lax.fori_loop(0, NC, turn, 0)

    def pair(k, _):
        both(2 * k, tab[AT_CEN, shot * NE + 2 * k], d0, d1)
        both(2 * k + 1, tab[AT_CEN, shot * NE + 2 * k + 1], d1, d0)
        return 0

    lax.fori_loop(1, NE // 2, pair, 0)
    acc[...] = jnp.zeros_like(acc)

    def last(i, _):
        mm_piece(NE - 1, d1, i, l_scr, acc)
        return 0

    lax.fori_loop(0, 8, last, 0)
    share(NE - 1)
    tiles[LIVE] = jnp.zeros((128, 128), BF16)

    def arrive(e, _):
        for d in range(1, NS):
            tile_copy(e, d).wait_recv()
        return 0

    lax.fori_loop(0, NE, arrive, 0)

    def owner_copy(d):
        g = lax.rem(beam + d, NG)
        return pltpu.make_async_remote_copy(
            src_ref=dense.at[g], dst_ref=got.at[beam], send_sem=ows.at[d], recv_sem=owr.at[d], **at_beam(g)
        )

    def gather_owner(d, _):
        g = lax.rem(beam + d, NG)
        s = tiles[tab[AT_PICK, g * NC]].astype(F32)
        for m in range(1, NC):
            s = s + tiles[tab[AT_PICK, g * NC + m]].astype(F32)
        dense[g] = s.astype(BF16)
        owner_copy(d).start()
        return 0

    lax.fori_loop(1, NG, gather_owner, 0)
    s = tiles[tab[AT_PICK, beam * NC]].astype(F32)
    for m in range(1, NC):
        s = s + tiles[tab[AT_PICK, beam * NC + m]].astype(F32)
    got[beam] = s.astype(BF16)

    for d in range(1, NG):
        trace_copy(d).wait_send()
    for cp in sends:
        cp.wait_send()

    def drain(e, _):
        for d in range(1, NS):
            depth_copy(e, d).wait_send()
            tile_copy(e, d).wait_send()
        return 0

    lax.fori_loop(0, NE, drain, 0)
    for e in range(EARLY):
        for d in range(1, NS):
            early_copy(e, d).wait_send()
    for slot in range(4):
        out_ref[slot] = jnp.zeros((128, 128), F32)

    for d in range(1, NG):
        owner_copy(d).wait_recv()

    def place(g, _):
        v = got[g].astype(F32)
        at = tab[AT_SLOT, g * NC]
        for c in range(1, NC):
            at = jnp.maximum(at, tab[AT_SLOT, g * NC + c])
        for slot in range(4):
            out_ref[slot] += v * jnp.where(at == slot, 1.0, 0.0)
        return 0

    lax.fori_loop(0, NG, place, 0)
    for d in range(1, NG):
        owner_copy(d).wait_send()


def fused(tab, traces, send, win, depth, lat, spr):
    t0, t1 = stack_tables()
    vm = pl.BlockSpec(memory_space=pltpu.VMEM)
    hbm = pl.BlockSpec(memory_space=pl.ANY)
    dma = pltpu.SemaphoreType.DMA
    return pl.pallas_call(
        kernel,
        out_shape=jax.ShapeDtypeStruct((4, 128, 128), F32),
        in_specs=[pl.BlockSpec(memory_space=pltpu.SMEM), vm, vm, vm, hbm, hbm, hbm, hbm, hbm],
        out_specs=vm,
        scratch_shapes=[
            pltpu.VMEM((WIN, NP, 128), BF16), pltpu.VMEM((WIN, NP, 128), BF16),
            pltpu.VMEM((256, 32, 128), F32), pltpu.VMEM((256, 32, 128), F32), pltpu.VMEM((256, 32, 128), F32),
            pltpu.VMEM((NG, 16, 128), BF16), pltpu.VMEM((NG, 16, 128), BF16),
            pltpu.VMEM((NC, WIN, 128), F32), pltpu.VMEM((NC, WIN, 128), F32),
            pltpu.VMEM((NS, NC, NP, 128), F32), pltpu.VMEM((NC, NP, 128), F32), pltpu.VMEM((NS, EARLY, NP, 128), F32), pltpu.VMEM((EARLY, NS, NP, 128), F32),
            pltpu.VMEM((NC + EARLY, 2, 128, 128), F32),
            pltpu.VMEM((NS, NE, NP, 128), F32), pltpu.VMEM((NE, NS, NP, 128), F32), pltpu.VMEM((2, 128, 128), F32),
            pltpu.VMEM((NF, 2, 128, 128), BF16), pltpu.VMEM((NF, 2, 128, 128), BF16),
            pltpu.VMEM((NE, 2, NF, NP, 128), BF16), pltpu.VMEM((128, 128), F32),
            pltpu.VMEM((LIVE + 1, 128, 128), BF16), pltpu.VMEM((NG, 128, 128), BF16), pltpu.VMEM((NG, 128, 128), BF16),
            dma((5,)), dma((NG,)), dma((NG,)), dma((7,)), dma((7,)), dma((EARLY, NS)), dma((EARLY, NS)),
            dma((NE, NS)), dma((NE, NS)), dma((NE, NS)), dma((NE, NS)), dma((NG,)), dma((NG,)),
        ],
        compiler_params=pltpu.CompilerParams(
            collective_id=0, has_side_effects=True, vmem_limit_bytes=62 * 1024 * 1024
        ),
        name="beam_migration",
    )(tab, traces, send, win, jnp.asarray(t0), jnp.asarray(t1), depth, lat, spr)


def body(traces, send_table, window_slots, ray_depth, ray_lateral, ray_spread, ray_index, foot_count, foot_tiles, tile_owner):
    tab = prep(foot_count, ray_index, foot_tiles, tile_owner)
    return fused(tab, traces[0], send_table[0], window_slots[0], ray_depth[0], ray_lateral, ray_spread)


def solution(mesh):
    in_specs = (
        P("shot", "beam", None),
        P("shot", None, None, None),
        P("shot", "beam", None),
        P("shot", "beam", None, None),
        P("beam", None, None),
        P("beam", None, None),
        P("beam", None),
        P("beam", None),
        P(),
        P(),
    )
    return jax.shard_map(body, mesh=mesh, in_specs=in_specs, out_specs=P(("shot", "beam"), None, None), check_vma=False)
```

```python
import math

import jax
import jax.numpy as jnp
import numpy as np
from jax import lax
from jax.experimental import pallas as pl
from jax.experimental.pallas import tpu as pltpu
from jax.sharding import PartitionSpec as P

MESH = pl.DeviceIdType.MESH
F32, BF16 = jnp.float32, jnp.bfloat16
NF, NP, NC, WIN, FOOT, LIVE = 64, 32, 8, 32, 12, 80
NS, NG, NE = 8, 16, 10
W0, DW, MID = 4.0, 60.0 / 64, 32
TWO_PI = 2.0 * math.pi
KP = 16
EARLY = 2
AT_ROW, AT_CEN, AT_PICK, AT_SLOT = 0, 1, 2, 3


def fit():
    x = np.cos(np.pi * (np.arange(400) + 0.5) / 400)
    q = (x * 0.5 + 0.5) * 0.25
    a = 2 * np.pi * np.sqrt(q)

    def poly(y, deg):
        c = np.polynomial.chebyshev.Chebyshev.fit(q, y, deg, domain=[0, 0.25])
        return [float(v) for v in c.convert(kind=np.polynomial.Polynomial).coef]

    return poly(np.cos(a), 7), poly(np.sin(a) / np.sqrt(q), 6)


COS_C, SIN_C = fit()


def sincos_turns(t):
    r = t - jnp.round(t)
    q = r * r
    cs = COS_C[-1]
    for c in COS_C[-2::-1]:
        cs = cs * q + c
    sn = SIN_C[-1]
    for c in SIN_C[-2::-1]:
        sn = sn * q + c
    return cs, sn * r


def stack_tables():
    f32 = np.float32
    angular = (2.0 * math.pi * (4.0 + 60.0 * np.arange(NF, dtype=f32) / NF)).astype(f32)
    centred = np.arange(WIN, dtype=f32) - f32(0.5 * (WIN - 1))
    taper = (np.exp(-((centred / f32(8.0)) ** 2)) / f32(math.sqrt(WIN))).astype(f32)
    slow = (f32(2e-05) * (np.arange(NP, dtype=f32) - f32(15.5))).astype(f32)
    angle = (angular[None, None, :] * slow[None, :, None]) * (f32(25.0) * centred)[:, None, None]
    sr = (taper[:, None, None] * np.cos(angle)).astype(BF16)
    si = (-taper[:, None, None] * np.sin(angle)).astype(BF16)
    return np.concatenate([sr, sr], 2), np.concatenate([-si, si], 2)


def lateral(tl, sp, l_scr, e):
    lc, ls = sincos_turns(W0 * tl)
    dm = jnp.exp(sp * (-TWO_PI * W0))
    lr, li = lc * dm, -(ls * dm)
    uc, us = sincos_turns(DW * tl)
    du = jnp.exp(sp * (-TWO_PI * DW))
    ur, ui = uc * du, -(us * du)
    for f in range(NF):
        l_scr[e, 0, f] = lr.astype(BF16)
        l_scr[e, 1, f] = li.astype(BF16)
        if f < NF - 1:
            lr, li = lr * ur - li * ui, lr * ui + li * ur


def depth_unit(c, d_scr, i, tdt, bt):
    z = pl.ds(pl.multiple_of(i * 16, 16), 16)
    seeds = []
    for h in range(2):
        t = tdt[h, z, :]
        c1, s1 = sincos_turns((W0 + DW * MID) * t)
        uc, us = sincos_turns(DW * t)
        seeds.append((c1 * uc + s1 * us, s1 * uc - c1 * us, c1, s1, uc + uc))

    def emit(f, st):
        ar = ai = None
        for h in range(2):
            br = bt[c, h, f : f + 1, :]
            bi = bt[c, h, NF + f : NF + f + 1, :]
            cv, sv = st[h][2], st[h][3]
            xr = br * cv - bi * sv
            xi = br * sv + bi * cv
            ar = xr if ar is None else ar + xr
            ai = xi if ai is None else ai + xi
        d_scr[f, 0, z, :] = ar.astype(BF16)
        d_scr[f, 1, z, :] = ai.astype(BF16)

    def step(st):
        return [(x[2], x[3], s[4] * x[2] - x[0], s[4] * x[3] - x[1]) for x, s in zip(st, seeds)]

    st = [s[:4] for s in seeds]
    for f in range(MID, NF):
        emit(f, st)
        if f < NF - 1:
            st = step(st)
    st = [(s[2], s[3], s[0], s[1]) for s in seeds]
    for f in range(MID - 1, -1, -1):
        emit(f, st)
        if f > 0:
            st = step(st)


def mm_piece(e, d_scr, i, l_scr, acc):
    part = i % 2
    f0 = (i // 2) * KP
    l8 = l_scr[e, part, pl.ds(f0, KP)]
    rhs = jnp.concatenate([l8[j] for j in range(KP) for _ in range(4)], 0)
    lhs = jnp.concatenate([d_scr[f0 + j, part] for j in range(KP)], 1)
    acc[...] += jnp.dot(lhs, rhs, preferred_element_type=F32)


def row_to_col(row):
    return jnp.broadcast_to(row, (128, 128)).T


def prep_kernel(count, index, foot, foot_v, owner_v, out_ref):
    shot = lax.axis_index("shot")
    beam = lax.axis_index("beam")
    n = lax.broadcasted_iota(jnp.int32, (1, 128), 1)
    cen = jnp.zeros((1, 128), jnp.int32)
    base = jnp.zeros((1, 128), jnp.int32)
    total = jnp.int32(0)
    for c in range(NC):
        prior = total
        total = total + count[0, c]
        cen = cen + jnp.where(n >= total, 1, 0)
        base = jnp.where(n >= prior, prior, base)
    eid = cen * FOOT + n - base
    rows = jnp.zeros((1, 128), jnp.int32)
    tile = jnp.zeros((1, 128), jnp.int32)
    for c in range(NC):
        for k in range(FOOT):
            hit = eid == c * FOOT + k
            rows = jnp.where(hit, index[c, k], rows)
            tile = jnp.where(hit, foot[beam * NC + c, k], tile)
    live = n < LIVE
    down = lax.broadcasted_iota(jnp.int32, (128, 128), 0).astype(F32)
    across = lax.broadcasted_iota(jnp.int32, (128, 128), 1).astype(F32)
    tile = tile.astype(F32)
    owners = owner_v[...].astype(F32)
    owner = jnp.zeros((1, 128), F32)
    for q in range(OWN_ROWS):
        hit = down + 128.0 * q == tile
        owner = owner + jnp.sum(jnp.where(hit, row_to_col(owners[q : q + 1]), 0.0), axis=0, keepdims=True)
    owner = jnp.where(live, owner, -1.0)
    same = (row_to_col(owner) == owner) & (down < across)
    rank = jnp.sum(jnp.where(same, 1.0, 0.0), axis=0, keepdims=True)
    key = jnp.where(live, (owner - (shot * NG).astype(F32)) * NC + rank, -1.0)
    hit = row_to_col(key) == across
    picks = LIVE + jnp.sum(jnp.where(hit, down - LIVE, 0.0), axis=0, keepdims=True)
    me = (shot * NG + beam).astype(F32)
    number = (
        lax.broadcasted_iota(jnp.int32, (OWN_ROWS, 128), 0) * 128 + lax.broadcasted_iota(jnp.int32, (OWN_ROWS, 128), 1)
    ).astype(F32)
    held = owners == me
    named = foot_v[...].astype(F32)
    slot = jnp.zeros(named.shape, F32)
    at = jnp.full((1, 1), -1.0, F32)
    for i in range(4):
        left = jnp.where(held & (number > at), number, 1e6)
        at = jnp.min(jnp.min(left, axis=0, keepdims=True), axis=1, keepdims=True)
        slot = jnp.where(named == at, float(i), slot)
    slot = jnp.max(slot, axis=1, keepdims=True)
    slot = jnp.broadcast_to(slot, (slot.shape[0], 128))
    if slot.shape[0] < 128:
        slot = jnp.concatenate([slot, jnp.zeros((128 - slot.shape[0], 128), F32)], 0)
    slot = slot.T[0:1]
    out_ref[...] = jnp.zeros((8, 128), jnp.int32)
    out_ref[AT_ROW : AT_ROW + 1] = rows
    out_ref[AT_CEN : AT_CEN + 1] = jnp.minimum(cen, NC - 1)
    out_ref[AT_PICK : AT_PICK + 1] = picks.astype(jnp.int32)
    out_ref[AT_SLOT : AT_SLOT + 1] = slot.astype(jnp.int32)


OWN_ROWS = NS * NG * 4 // 128


def prep(foot_count, ray_index, foot_tiles, tile_owner):
    vm, sm = pl.BlockSpec(memory_space=pltpu.VMEM), pl.BlockSpec(memory_space=pltpu.SMEM)
    return pl.pallas_call(
        prep_kernel,
        out_shape=jax.ShapeDtypeStruct((8, 128), jnp.int32),
        in_specs=[sm, sm, sm, vm, vm],
        out_specs=vm,
        name="entry_table",
    )(foot_count, ray_index, foot_tiles, foot_tiles, tile_owner.reshape(OWN_ROWS, 128))


def one_hot(x, count, width):
    xt = jnp.concatenate([x.astype(F32), jnp.zeros((x.shape[0], 128 - count), F32)], 1).T
    lanes = lax.broadcasted_iota(jnp.int32, (count, width), 1).astype(F32)
    parts = [jnp.where(lanes == xt[:count, r : r + 1], 1.0, 0.0) for r in range(x.shape[0])]
    return jnp.concatenate(parts, 0).astype(BF16)


def kernel(
    tab, traces, send_ref, win_ref, t0_hbm, t1_hbm, depth_hbm, lat_hbm, spr_hbm, out_ref,
    t0, t1, depth_v, lat_v, spr_v, tr_out, tr_in, win_s, win_r, ball, b_own, b_out, b_in, bt, td_out, td_in, tdt,
    d0, d1, l_scr, acc, tiles, dense, got,
    tab_sem, trs, trr, bs, br_sem, bes, ber, tds, tdr, tls, tlr, ows, owr,
):
    shot = lax.axis_index("shot")
    beam = lax.axis_index("beam")
    way = 1 - 2 * lax.rem(shot, 2)
    partner = shot + way
    ahead = lax.rem(shot + 2 * way + NS, NS)
    behind = lax.rem(shot - 2 * way + NS, NS)
    ring = (
        (shot, ahead), (shot, behind), (shot, partner),
        (behind, ahead), (behind, ahead + way), (behind, partner), (ahead, partner),
    )

    def at_shot(s):
        return dict(device_id={"shot": s, "beam": beam}, device_id_type=MESH)

    def at_beam(g):
        return dict(device_id={"shot": shot, "beam": g}, device_id_type=MESH)

    def await_all(ref, sem):
        pltpu.make_async_copy(ref, ref, sem).wait()

    barrier = pltpu.get_barrier_semaphore()
    for d in range(1, NG):
        pl.semaphore_signal(barrier, inc=1, **at_beam(lax.rem(beam + d, NG)))
    for d in range(1, NS):
        pl.semaphore_signal(barrier, inc=1, **at_shot(lax.rem(shot + d, NS)))
    pairs = ((depth_hbm, depth_v), (lat_hbm, lat_v), (spr_hbm, spr_v), (t0_hbm, t0), (t1_hbm, t1))
    loads = [pltpu.make_async_copy(h, v, tab_sem.at[n]) for n, (h, v) in enumerate(pairs)]
    for cp in loads:
        cp.start()

    pick = one_hot(send_ref[beam], 16, 256)
    chosen = jnp.dot(pick, traces[...], preferred_element_type=F32).astype(BF16)
    tr_out[...] = chosen.reshape(NG, 16, 128)
    tr_in[beam] = tr_out[beam]
    pl.semaphore_wait(barrier, NS - 1 + NG - 1)

    def trace_copy(d):
        g = lax.rem(beam + d, NG)
        return pltpu.make_async_remote_copy(
            src_ref=tr_out.at[g], dst_ref=tr_in.at[beam], send_sem=trs, recv_sem=trr, **at_beam(g)
        )

    for d in range(1, NG):
        trace_copy(d).start()

    loads[0].wait()

    def gather(e, _):
        for j in range(NS):
            td_out[j, e] = depth_v[tab[AT_ROW, j * NE + e]]
        td_in[e, shot] = depth_v[tab[AT_ROW, shot * NE + e]]
        return 0

    lax.fori_loop(0, NE, gather, 0)

    def depth_copy(e, d):
        j = lax.rem(shot + d, NS)
        return pltpu.make_async_remote_copy(
            src_ref=td_out.at[j, e], dst_ref=td_in.at[e, shot], send_sem=tds, recv_sem=tdr.at[e], **at_shot(j)
        )

    for d in range(1, NS):
        depth_copy(0, d).start()
    loads[1].wait()
    loads[2].wait()

    def lat(e, _):
        r = tab[AT_ROW, shot * NE + e]
        lateral(lat_v[r], spr_v[r], l_scr, e)
        return 0

    lax.fori_loop(0, NE // 2, lat, 0)
    pick = one_hot(win_ref[...], WIN, NG * 16)
    loads[3].wait()
    loads[4].wait()

    await_all(tr_in.at[0 : NG - 1], trr)
    win = jnp.dot(pick, tr_in[...].reshape(NG * 16, 128), preferred_element_type=F32)
    win_s[...] = win.reshape(NC, WIN, 128)
    win_r[...] = pltpu.roll(win, 64, 1).reshape(NC, WIN, 128)

    def stack(c, _):
        a = jnp.zeros((NP, 128), F32)
        for k in range(WIN):
            a = a + (t0[k].astype(F32) * win_s[c, k : k + 1, :] + t1[k].astype(F32) * win_r[c, k : k + 1, :])
        b_own[c] = a * (1.0 / math.sqrt(NP * NF))
        return 0

    lax.fori_loop(0, NC, stack, 0)

    def early_copy(e, d):
        j = lax.rem(shot + d, NS)
        return pltpu.make_async_remote_copy(
            src_ref=b_out.at[j, e], dst_ref=b_in.at[e, shot], send_sem=bes, recv_sem=ber.at[e], **at_shot(j)
        )

    for e in range(EARLY):
        for j in range(NS):
            b_out[j, e] = b_own[tab[AT_CEN, j * NE + e]]
        b_in[e, shot] = b_own[tab[AT_CEN, shot * NE + e]]

    def beam_copy(n):
        item, to = ring[n]
        return pltpu.make_async_remote_copy(
            src_ref=b_own if n < 3 else ball.at[item], dst_ref=ball.at[item],
            send_sem=bs.at[n], recv_sem=br_sem.at[n], **at_shot(to),
        )

    def tile_copy(e, d):
        n = shot * NE + e
        return pltpu.make_async_remote_copy(
            src_ref=tiles.at[n], dst_ref=tiles.at[n], send_sem=tls, recv_sem=tlr, **at_shot(lax.rem(shot + d, NS))
        )

    def early_send(e):
        for d in range(1, NS):
            early_copy(e, d).start()

    def depth_send(e):
        for d in range(1, NS):
            depth_copy(e, d).start()

    early_send(0)
    for n in range(3):
        beam_copy(n).start()
    depth_send(1)
    for e in range(1, EARLY):
        early_send(e)
    ball[shot] = b_own[...]
    lax.fori_loop(NE // 2, NE, lat, 0)

    def share(e):
        tiles[shot * NE + e] = acc[...].astype(BF16)
        for d in range(1, NS):
            tile_copy(e, d).start()

    def both(e, c, dst, src, after=None):
        await_all(td_in.at[e, 0 : NS - 1], tdr.at[e])
        for h in range(2):
            tdt[h] = td_in[e, 4 * h : 4 * h + 4].reshape(128, 128).T
        acc[...] = jnp.zeros_like(acc)

        def unit(i, _):
            if src is not None:
                mm_piece(e - 1, src, i, l_scr, acc)
            depth_unit(c, dst, i, tdt, bt)
            return 0

        lax.fori_loop(0, 8, unit, 0)
        if src is not None:
            share(e - 1)
        if after is not None:
            after()
        if isinstance(e, int):
            depth_send(e + 2)
        else:

            @pl.when(e + 2 < NE)
            def _():
                depth_send(e + 2)

    def early(e):
        await_all(b_in.at[e, 0 : NS - 1], ber.at[e])
        for h in range(2):
            bt[NC + e, h] = b_in[e, 4 * h : 4 * h + 4].reshape(128, 128).T

    def pass_beams():
        for n in range(2):
            beam_copy(n).wait_recv()
        for n in range(3, 7):
            beam_copy(n).start()

    early(0)
    both(0, NC, d0, None, pass_beams)
    early(1)
    both(1, NC + 1, d1, d0)
    for n in range(2, 7):
        beam_copy(n).wait_recv()

    def turn(c, _):
        for h in range(2):
            bt[c, h] = jnp.concatenate([ball[4 * h + s, c] for s in range(4)], 0).T
        return 0

    lax.fori_loop(0, NC, turn, 0)

    def pair(k, _):
        both(2 * k, tab[AT_CEN, shot * NE + 2 * k], d0, d1)
        both(2 * k + 1, tab[AT_CEN, shot * NE + 2 * k + 1], d1, d0)
        return 0

    lax.fori_loop(1, NE // 2, pair, 0)
    acc[...] = jnp.zeros_like(acc)

    def last(i, _):
        mm_piece(NE - 1, d1, i, l_scr, acc)
        return 0

    lax.fori_loop(0, 8, last, 0)
    share(NE - 1)
    tiles[LIVE] = jnp.zeros((128, 128), BF16)

    await_all(tiles.at[0 : LIVE - NE], tlr)

    def owner_copy(d):
        g = lax.rem(beam + d, NG)
        return pltpu.make_async_remote_copy(
            src_ref=dense.at[g], dst_ref=got.at[beam], send_sem=ows, recv_sem=owr, **at_beam(g)
        )

    def gather_owner(d, _):
        g = lax.rem(beam + d, NG)
        s = tiles[tab[AT_PICK, g * NC]].astype(F32)
        for m in range(1, NC):
            s = s + tiles[tab[AT_PICK, g * NC + m]].astype(F32)
        dense[g] = s.astype(BF16)
        owner_copy(d).start()
        return 0

    lax.fori_loop(1, NG, gather_owner, 0)
    s = tiles[tab[AT_PICK, beam * NC]].astype(F32)
    for m in range(1, NC):
        s = s + tiles[tab[AT_PICK, beam * NC + m]].astype(F32)
    got[beam] = s.astype(BF16)

    await_all(tr_out.at[0 : NG - 1], trs)
    for n in range(7):
        beam_copy(n).wait_send()

    await_all(td_out.at[0 : NS - 1], tds)
    await_all(tiles.at[0 : LIVE - NE], tls)
    await_all(b_out.at[0 : NS - 1], bes)
    for slot in range(4):
        out_ref[slot] = jnp.zeros((128, 128), F32)

    await_all(got.at[0 : NG - 1], owr)

    def place(g, _):
        v = got[g].astype(F32)
        at = tab[AT_SLOT, g * NC]
        for c in range(1, NC):
            at = jnp.maximum(at, tab[AT_SLOT, g * NC + c])
        for slot in range(4):
            out_ref[slot] += v * jnp.where(at == slot, 1.0, 0.0)
        return 0

    lax.fori_loop(0, NG, place, 0)
    await_all(dense.at[0 : NG - 1], ows)


def fused(tab, traces, send, win, depth, lat, spr):
    t0, t1 = stack_tables()
    vm = pl.BlockSpec(memory_space=pltpu.VMEM)
    hbm = pl.BlockSpec(memory_space=pl.ANY)
    dma = pltpu.SemaphoreType.DMA
    return pl.pallas_call(
        kernel,
        out_shape=jax.ShapeDtypeStruct((4, 128, 128), F32),
        in_specs=[pl.BlockSpec(memory_space=pltpu.SMEM), vm, vm, vm, hbm, hbm, hbm, hbm, hbm],
        out_specs=vm,
        scratch_shapes=[
            pltpu.VMEM((WIN, NP, 128), BF16), pltpu.VMEM((WIN, NP, 128), BF16),
            pltpu.VMEM((256, 32, 128), F32), pltpu.VMEM((256, 32, 128), F32), pltpu.VMEM((256, 32, 128), F32),
            pltpu.VMEM((NG, 16, 128), BF16), pltpu.VMEM((NG, 16, 128), BF16),
            pltpu.VMEM((NC, WIN, 128), F32), pltpu.VMEM((NC, WIN, 128), F32),
            pltpu.VMEM((NS, NC, NP, 128), F32), pltpu.VMEM((NC, NP, 128), F32), pltpu.VMEM((NS, EARLY, NP, 128), F32), pltpu.VMEM((EARLY, NS, NP, 128), F32),
            pltpu.VMEM((NC + EARLY, 2, 128, 128), F32),
            pltpu.VMEM((NS, NE, NP, 128), F32), pltpu.VMEM((NE, NS, NP, 128), F32), pltpu.VMEM((2, 128, 128), F32),
            pltpu.VMEM((NF, 2, 128, 128), BF16), pltpu.VMEM((NF, 2, 128, 128), BF16),
            pltpu.VMEM((NE, 2, NF, NP, 128), BF16), pltpu.VMEM((128, 128), F32),
            pltpu.VMEM((LIVE + 1, 128, 128), BF16), pltpu.VMEM((NG, 128, 128), BF16), pltpu.VMEM((NG, 128, 128), BF16),
            dma((5,)), dma(()), dma(()), dma((7,)), dma((7,)), dma(()), dma((EARLY,)),
            dma(()), dma((NE,)), dma(()), dma(()), dma(()), dma(()),
        ],
        compiler_params=pltpu.CompilerParams(
            collective_id=0, has_side_effects=True, vmem_limit_bytes=62 * 1024 * 1024
        ),
        name="beam_migration",
    )(tab, traces, send, win, jnp.asarray(t0), jnp.asarray(t1), depth, lat, spr)


def body(traces, send_table, window_slots, ray_depth, ray_lateral, ray_spread, ray_index, foot_count, foot_tiles, tile_owner):
    tab = prep(foot_count, ray_index, foot_tiles, tile_owner)
    return fused(tab, traces[0], send_table[0], window_slots[0], ray_depth[0], ray_lateral, ray_spread)


def solution(mesh):
    in_specs = (
        P("shot", "beam", None),
        P("shot", None, None, None),
        P("shot", "beam", None),
        P("shot", "beam", None, None),
        P("beam", None, None),
        P("beam", None, None),
        P("beam", None),
        P("beam", None),
        P(),
        P(),
    )
    return jax.shard_map(body, mesh=mesh, in_specs=in_specs, out_specs=P(("shot", "beam"), None, None), check_vma=False)
```

```python
import functools
import math

import jax
import jax.numpy as jnp
import numpy as np
from jax import lax
from jax.experimental import pallas as pl
from jax.experimental.pallas import tpu as pltpu
from jax.sharding import PartitionSpec as P

MESH = pl.DeviceIdType.MESH
F32, BF16 = jnp.float32, jnp.bfloat16
NF, NP, NC, WIN, FOOT, LIVE = 64, 32, 8, 32, 12, 80
NS, NG, NE = 8, 16, 10
W0, DW, MID = 4.0, 60.0 / 64, 32
TWO_PI = 2.0 * math.pi
KP = 16
EARLY = 2
AT_ROW, AT_CEN, AT_PICK, AT_SLOT = 0, 1, 2, 3


def fit():
    x = np.cos(np.pi * (np.arange(400) + 0.5) / 400)
    q = (x * 0.5 + 0.5) * 0.25
    a = 2 * np.pi * np.sqrt(q)

    def poly(y, deg):
        c = np.polynomial.chebyshev.Chebyshev.fit(q, y, deg, domain=[0, 0.25])
        return [float(v) for v in c.convert(kind=np.polynomial.Polynomial).coef]

    return poly(np.cos(a), 7), poly(np.sin(a) / np.sqrt(q), 6)


COS_C, SIN_C = fit()


def sincos_turns(t):
    r = t - jnp.round(t)
    q = r * r
    cs = COS_C[-1]
    for c in COS_C[-2::-1]:
        cs = cs * q + c
    sn = SIN_C[-1]
    for c in SIN_C[-2::-1]:
        sn = sn * q + c
    return cs, sn * r


def stack_tables():
    f32 = np.float32
    angular = (2.0 * math.pi * (4.0 + 60.0 * np.arange(NF, dtype=f32) / NF)).astype(f32)
    centred = np.arange(WIN, dtype=f32) - f32(0.5 * (WIN - 1))
    taper = (np.exp(-((centred / f32(8.0)) ** 2)) / f32(math.sqrt(WIN))).astype(f32)
    slow = (f32(2e-05) * (np.arange(NP, dtype=f32) - f32(15.5))).astype(f32)
    angle = (angular[None, None, :] * slow[None, :, None]) * (f32(25.0) * centred)[:, None, None]
    sr = (taper[:, None, None] * np.cos(angle)).astype(BF16)
    si = (-taper[:, None, None] * np.sin(angle)).astype(BF16)
    return np.concatenate([sr, sr], 2), np.concatenate([-si, si], 2)


def lateral(tl, sp, l_scr, e):
    lc, ls = sincos_turns(W0 * tl)
    dm = jnp.exp(sp * (-TWO_PI * W0))
    lr, li = lc * dm, -(ls * dm)
    uc, us = sincos_turns(DW * tl)
    du = jnp.exp(sp * (-TWO_PI * DW))
    ur, ui = uc * du, -(us * du)
    for f in range(NF):
        l_scr[e, 0, f] = lr.astype(BF16)
        l_scr[e, 1, f] = li.astype(BF16)
        if f < NF - 1:
            lr, li = lr * ur - li * ui, lr * ui + li * ur


def depth_unit(c, d_scr, i, tdt, bt):
    z = pl.ds(pl.multiple_of(i * 16, 16), 16)
    seeds = []
    for h in range(2):
        t = tdt[h, z, :]
        c1, s1 = sincos_turns((W0 + DW * MID) * t)
        uc, us = sincos_turns(DW * t)
        seeds.append((c1 * uc + s1 * us, s1 * uc - c1 * us, c1, s1, uc + uc))

    def emit(f, st):
        ar = ai = None
        for h in range(2):
            br = bt[c, h, f : f + 1, :]
            bi = bt[c, h, NF + f : NF + f + 1, :]
            cv, sv = st[h][2], st[h][3]
            xr = br * cv - bi * sv
            xi = br * sv + bi * cv
            ar = xr if ar is None else ar + xr
            ai = xi if ai is None else ai + xi
        d_scr[f, 0, z, :] = ar.astype(BF16)
        d_scr[f, 1, z, :] = ai.astype(BF16)

    def step(st):
        return [(x[2], x[3], s[4] * x[2] - x[0], s[4] * x[3] - x[1]) for x, s in zip(st, seeds)]

    st = [s[:4] for s in seeds]
    for f in range(MID, NF):
        emit(f, st)
        if f < NF - 1:
            st = step(st)
    st = [(s[2], s[3], s[0], s[1]) for s in seeds]
    for f in range(MID - 1, -1, -1):
        emit(f, st)
        if f > 0:
            st = step(st)


def mm_piece(e, d_scr, i, l_scr, accs):
    part = i % 2
    f0 = (i // 2) * KP
    blank = jnp.zeros((256, 128), BF16)
    for t in range(KP // 2):
        unit = t % 2
        f = f0 + 2 * t
        la, lb = l_scr[e, part, f], l_scr[e, part, f + 1]
        rhs = jnp.concatenate([jnp.concatenate([la] * 4 + [lb] * 4, 0), blank], 1)
        stage = (t // 2) % 2
        pltpu.matmul_push_rhs(rhs, stage, unit)
        lhs = jnp.concatenate([d_scr[f, part], d_scr[f + 1, part]], 1)
        pltpu.matmul_acc_lhs(accs[unit], lhs, load_staged_rhs=stage)


def mm_result(accs):
    return pltpu.matmul_pop(accs[0])[:, :128] + pltpu.matmul_pop(accs[1])[:, :128]


def row_to_col(row):
    return jnp.broadcast_to(row, (128, 128)).T


def prep_kernel(count, index, foot, foot_v, owner_v, out_ref):
    shot = lax.axis_index("shot")
    beam = lax.axis_index("beam")
    n = lax.broadcasted_iota(jnp.int32, (1, 128), 1)
    cen = jnp.zeros((1, 128), jnp.int32)
    base = jnp.zeros((1, 128), jnp.int32)
    total = jnp.int32(0)
    for c in range(NC):
        prior = total
        total = total + count[0, c]
        cen = cen + jnp.where(n >= total, 1, 0)
        base = jnp.where(n >= prior, prior, base)
    eid = cen * FOOT + n - base
    rows = jnp.zeros((1, 128), jnp.int32)
    tile = jnp.zeros((1, 128), jnp.int32)
    for c in range(NC):
        for k in range(FOOT):
            hit = eid == c * FOOT + k
            rows = jnp.where(hit, index[c, k], rows)
            tile = jnp.where(hit, foot[k, beam * NC + c], tile)
    live = n < LIVE
    down = lax.broadcasted_iota(jnp.int32, (128, 128), 0).astype(F32)
    across = lax.broadcasted_iota(jnp.int32, (128, 128), 1).astype(F32)
    tile = tile.astype(F32)
    owners = owner_v[...].astype(F32)
    owner = jnp.zeros((1, 128), F32)
    for q in range(OWN_ROWS):
        hit = down + 128.0 * q == tile
        owner = owner + jnp.sum(jnp.where(hit, row_to_col(owners[q : q + 1]), 0.0), axis=0, keepdims=True)
    owner = jnp.where(live, owner, -1.0)
    same = (row_to_col(owner) == owner) & (down < across)
    rank = jnp.sum(jnp.where(same, 1.0, 0.0), axis=0, keepdims=True)
    key = jnp.where(live, (owner - (shot * NG).astype(F32)) * NC + rank, -1.0)
    hit = row_to_col(key) == across
    picks = LIVE + jnp.sum(jnp.where(hit, down - LIVE, 0.0), axis=0, keepdims=True)
    me = (shot * NG + beam).astype(F32)
    number = (
        lax.broadcasted_iota(jnp.int32, (OWN_ROWS, 128), 0) * 128 + lax.broadcasted_iota(jnp.int32, (OWN_ROWS, 128), 1)
    ).astype(F32)
    held = owners == me
    named = foot_v[...].astype(F32)
    slot = jnp.zeros(named.shape, F32)
    at = jnp.full((1, 1), -1.0, F32)
    for i in range(4):
        left = jnp.where(held & (number > at), number, 1e6)
        at = jnp.min(jnp.min(left, axis=0, keepdims=True), axis=1, keepdims=True)
        slot = jnp.where(named == at, float(i), slot)
    slot = jnp.max(slot, axis=0, keepdims=True)
    out_ref[...] = jnp.zeros((8, 128), jnp.int32)
    out_ref[AT_ROW : AT_ROW + 1] = rows
    out_ref[AT_CEN : AT_CEN + 1] = jnp.minimum(cen, NC - 1)
    out_ref[AT_PICK : AT_PICK + 1] = picks.astype(jnp.int32)
    out_ref[AT_SLOT : AT_SLOT + 1] = slot.astype(jnp.int32)


OWN_ROWS = NS * NG * 4 // 128


def prep(foot_count, ray_index, foot_tiles, tile_owner):
    vm, sm = pl.BlockSpec(memory_space=pltpu.VMEM), pl.BlockSpec(memory_space=pltpu.SMEM)
    return pl.pallas_call(
        prep_kernel,
        out_shape=jax.ShapeDtypeStruct((8, 128), jnp.int32),
        in_specs=[sm, sm, sm, vm, vm],
        out_specs=vm,
        name="entry_table",
    )(foot_count, ray_index, foot_tiles.T, foot_tiles.T, tile_owner.reshape(OWN_ROWS, 128))


def one_hot(x, count, width):
    xt = jnp.concatenate([x.astype(F32), jnp.zeros((x.shape[0], 128 - count), F32)], 1).T
    lanes = lax.broadcasted_iota(jnp.int32, (count, width), 1).astype(F32)
    parts = [jnp.where(lanes == xt[:count, r : r + 1], 1.0, 0.0) for r in range(x.shape[0])]
    return jnp.concatenate(parts, 0).astype(BF16)


def kernel(
    mesh, tab, traces, send_ref, win_ref, t0_hbm, t1_hbm, depth_hbm, lat_hbm, spr_hbm, out_ref,
    t0, t1, depth_v, lat_v, spr_v, tr_out, tr_in, win_s, win_r, ball, b_own, b_out, b_in, bt, td_out, td_in, tdt,
    d0, d1, l_scr, tiles, dense, got,
    tab_sem, trs, trr, bs, br_sem, bes, ber, tds, tdr, tls, tln, tlr, ows, owr,
):
    shot = lax.axis_index("shot")
    beam = lax.axis_index("beam")
    way = 1 - 2 * lax.rem(shot, 2)
    partner = shot + way
    ahead = lax.rem(shot + 2 * way + NS, NS)
    behind = lax.rem(shot - 2 * way + NS, NS)
    ring = (
        (shot, ahead), (shot, behind), (shot, partner),
        (behind, ahead), (behind, ahead + way), (behind, partner), (ahead, partner),
    )

    def at_shot(s):
        return dict(device_id={"shot": s, "beam": beam}, device_id_type=MESH)

    def at_beam(g):
        return dict(device_id={"shot": shot, "beam": g}, device_id_type=MESH)

    def await_all(ref, sem):
        pltpu.make_async_copy(ref, ref, sem).wait()

    barrier = pltpu.get_barrier_semaphore()
    for d in range(1, NG):
        pl.semaphore_signal(barrier, inc=1, **at_beam(lax.rem(beam + d, NG)))
    for d in range(1, NS):
        pl.semaphore_signal(barrier, inc=1, **at_shot(lax.rem(shot + d, NS)))
    pairs = ((depth_hbm, depth_v), (lat_hbm, lat_v), (spr_hbm, spr_v), (t0_hbm, t0), (t1_hbm, t1))
    loads = [pltpu.make_async_copy(h, v, tab_sem.at[n]) for n, (h, v) in enumerate(pairs)]
    for cp in loads:
        cp.start()

    def select(pick, rows):
        def go(total):
            wide = jnp.concatenate([rows, jnp.zeros((256, 128), BF16)], 1)
            pltpu.matmul_push_rhs(wide, 0, 0)
            pltpu.matmul_acc_lhs(total, pick, load_staged_rhs=0)
            return pltpu.matmul_pop(total)[:, :128]

        with jax.sharding.use_abstract_mesh(mesh.abstract_mesh):
            kind = pltpu.ACC(0)((256, 256), F32)
        return pl.run_scoped(go, kind)

    pick = one_hot(send_ref[beam], 16, 256)
    chosen = select(pick, traces[...]).astype(BF16)
    tr_out[...] = chosen.reshape(NG, 16, 128)
    tr_in[beam] = tr_out[beam]
    pl.semaphore_wait(barrier, NS - 1 + NG - 1)

    def trace_copy(d):
        g = lax.rem(beam + d, NG)
        return pltpu.make_async_remote_copy(
            src_ref=tr_out.at[g], dst_ref=tr_in.at[beam], send_sem=trs, recv_sem=trr, **at_beam(g)
        )

    for d in range(1, NG):
        trace_copy(d).start()

    loads[0].wait()

    def gather(e, _):
        for j in range(NS):
            td_out[j, e] = depth_v[tab[AT_ROW, j * NE + e]]
        td_in[e, shot] = depth_v[tab[AT_ROW, shot * NE + e]]
        return 0

    lax.fori_loop(0, NE, gather, 0)

    def depth_copy(e, d):
        j = lax.rem(shot + d, NS)
        return pltpu.make_async_remote_copy(
            src_ref=td_out.at[j, e], dst_ref=td_in.at[e, shot], send_sem=tds, recv_sem=tdr.at[e], **at_shot(j)
        )

    for d in range(1, NS):
        depth_copy(0, d).start()
    loads[1].wait()
    loads[2].wait()

    def lat(e, _):
        r = tab[AT_ROW, shot * NE + e]
        lateral(lat_v[r], spr_v[r], l_scr, e)
        return 0

    lax.fori_loop(0, NE // 2, lat, 0)
    pick = one_hot(win_ref[...], WIN, NG * 16)
    loads[3].wait()
    loads[4].wait()

    await_all(tr_in.at[0 : NG - 1], trr)
    win = select(pick, tr_in[...].reshape(NG * 16, 128))
    win_s[...] = win.reshape(NC, WIN, 128)
    win_r[...] = pltpu.roll(win, 64, 1).reshape(NC, WIN, 128)

    def stack(c, _):
        a = jnp.zeros((NP, 128), F32)
        for k in range(WIN):
            a = a + (t0[k].astype(F32) * win_s[c, k : k + 1, :] + t1[k].astype(F32) * win_r[c, k : k + 1, :])
        b_own[c] = a * (1.0 / math.sqrt(NP * NF))
        return 0

    lax.fori_loop(0, NC, stack, 0)

    def early_copy(e, d):
        j = lax.rem(shot + d, NS)
        return pltpu.make_async_remote_copy(
            src_ref=b_out.at[j, e], dst_ref=b_in.at[e, shot], send_sem=bes, recv_sem=ber.at[e], **at_shot(j)
        )

    for e in range(EARLY):
        for j in range(NS):
            b_out[j, e] = b_own[tab[AT_CEN, j * NE + e]]
        b_in[e, shot] = b_own[tab[AT_CEN, shot * NE + e]]

    def beam_copy(n):
        item, to = ring[n]
        return pltpu.make_async_remote_copy(
            src_ref=b_own if n < 3 else ball.at[item], dst_ref=ball.at[item],
            send_sem=bs.at[n], recv_sem=br_sem.at[n], **at_shot(to),
        )

    def tile_copy(e, n):
        item, to = ring[n]
        return pltpu.make_async_remote_copy(
            src_ref=tiles.at[item * NE + e], dst_ref=tiles.at[item * NE + e],
            send_sem=tls, recv_sem=tln.at[e] if n < 2 else tlr, **at_shot(to),
        )

    def relay(e):
        await_all(tiles.at[0:2], tln.at[e])
        for n in range(3, 7):
            tile_copy(e, n).start()

    def early_send(e):
        for d in range(1, NS):
            early_copy(e, d).start()

    def depth_send(e):
        for d in range(1, NS):
            depth_copy(e, d).start()

    early_send(0)
    for n in range(3):
        beam_copy(n).start()
    depth_send(1)
    for e in range(1, EARLY):
        early_send(e)
    ball[shot] = b_own[...]
    lax.fori_loop(NE // 2, NE, lat, 0)

    def share(e, accs):
        tiles[shot * NE + e] = mm_result(accs).astype(BF16)
        for n in range(3):
            tile_copy(e, n).start()

    def both(accs, e, c, dst, src, after=None):
        await_all(td_in.at[e, 0 : NS - 1], tdr.at[e])
        for h in range(2):
            tdt[h] = td_in[e, 4 * h : 4 * h + 4].reshape(128, 128).T

        def unit(i, _):
            if src is not None:
                mm_piece(e - 1, src, i, l_scr, accs)
            depth_unit(c, dst, i, tdt, bt)
            return 0

        lax.fori_loop(0, 8, unit, 0)
        if src is not None:
            share(e - 1, accs)
        if after is not None:
            after()
        if isinstance(e, int):
            depth_send(e + 2)
        else:
            relay(e - 2)

            @pl.when(e + 2 < NE)
            def _():
                depth_send(e + 2)

    def early(e):
        await_all(b_in.at[e, 0 : NS - 1], ber.at[e])
        for h in range(2):
            bt[NC + e, h] = b_in[e, 4 * h : 4 * h + 4].reshape(128, 128).T

    def pass_beams():
        for n in range(2):
            beam_copy(n).wait_recv()
        for n in range(3, 7):
            beam_copy(n).start()

    def migrate(*accs):
        early(0)
        both(accs, 0, NC, d0, None, pass_beams)
        early(1)
        both(accs, 1, NC + 1, d1, d0)
        for n in range(2, 7):
            beam_copy(n).wait_recv()

        def turn(c, _):
            for h in range(2):
                bt[c, h] = jnp.concatenate([ball[4 * h + s, c] for s in range(4)], 0).T
            return 0

        lax.fori_loop(0, NC, turn, 0)

        def pair(k, _):
            both(accs, 2 * k, tab[AT_CEN, shot * NE + 2 * k], d0, d1)
            both(accs, 2 * k + 1, tab[AT_CEN, shot * NE + 2 * k + 1], d1, d0)
            return 0

        lax.fori_loop(1, NE // 2, pair, 0)

        def last(i, _):
            mm_piece(NE - 1, d1, i, l_scr, accs)
            return 0

        lax.fori_loop(0, 8, last, 0)
        share(NE - 1, accs)

    with jax.sharding.use_abstract_mesh(mesh.abstract_mesh):
        kinds = [pltpu.ACC(u)((128, 256), F32) for u in range(2)]
    pl.run_scoped(migrate, *kinds)
    relay(NE - 2)
    tiles[LIVE] = jnp.zeros((128, 128), BF16)
    relay(NE - 1)

    await_all(tiles.at[0 : 5 * NE], tlr)

    def owner_copy(d):
        g = lax.rem(beam + d, NG)
        return pltpu.make_async_remote_copy(
            src_ref=dense.at[g], dst_ref=got.at[beam], send_sem=ows, recv_sem=owr, **at_beam(g)
        )

    def gather_owner(d, _):
        g = lax.rem(beam + d, NG)
        s = tiles[tab[AT_PICK, g * NC]].astype(F32)
        for m in range(1, NC):
            s = s + tiles[tab[AT_PICK, g * NC + m]].astype(F32)
        dense[g] = s.astype(BF16)
        owner_copy(d).start()
        return 0

    lax.fori_loop(1, NG, gather_owner, 0)
    s = tiles[tab[AT_PICK, beam * NC]].astype(F32)
    for m in range(1, NC):
        s = s + tiles[tab[AT_PICK, beam * NC + m]].astype(F32)
    got[beam] = s.astype(BF16)

    await_all(tr_out.at[0 : NG - 1], trs)
    for n in range(7):
        beam_copy(n).wait_send()

    await_all(td_out.at[0 : NS - 1], tds)
    await_all(tiles.at[0 : LIVE - NE], tls)
    await_all(b_out.at[0 : NS - 1], bes)
    await_all(got.at[0 : NG - 1], owr)

    weights = []
    for g in range(NG):
        at = tab[AT_SLOT, g * NC]
        for c in range(1, NC):
            at = jnp.maximum(at, tab[AT_SLOT, g * NC + c])
        weights.append([jnp.where(at == slot, 1.0, 0.0) for slot in range(4)])

    def place(i, _):
        z = pl.ds(pl.multiple_of(i * 16, 16), 16)
        sums = [jnp.zeros((16, 128), F32)] * 4
        for g in range(NG):
            v = got[g, z, :].astype(F32)
            sums = [a + v * w for a, w in zip(sums, weights[g])]
        for slot in range(4):
            out_ref[slot, z, :] = sums[slot]
        return 0

    lax.fori_loop(0, 8, place, 0)
    await_all(dense.at[0 : NG - 1], ows)


def fused(mesh, tab, traces, send, win, depth, lat, spr):
    t0, t1 = stack_tables()
    vm = pl.BlockSpec(memory_space=pltpu.VMEM)
    hbm = pl.BlockSpec(memory_space=pl.ANY)
    dma = pltpu.SemaphoreType.DMA
    return pl.pallas_call(
        functools.partial(kernel, mesh),
        out_shape=jax.ShapeDtypeStruct((4, 128, 128), F32),
        in_specs=[pl.BlockSpec(memory_space=pltpu.SMEM), vm, vm, vm, hbm, hbm, hbm, hbm, hbm],
        out_specs=vm,
        scratch_shapes=[
            pltpu.VMEM((WIN, NP, 128), BF16), pltpu.VMEM((WIN, NP, 128), BF16),
            pltpu.VMEM((256, 32, 128), F32), pltpu.VMEM((256, 32, 128), F32), pltpu.VMEM((256, 32, 128), F32),
            pltpu.VMEM((NG, 16, 128), BF16), pltpu.VMEM((NG, 16, 128), BF16),
            pltpu.VMEM((NC, WIN, 128), F32), pltpu.VMEM((NC, WIN, 128), F32),
            pltpu.VMEM((NS, NC, NP, 128), F32), pltpu.VMEM((NC, NP, 128), F32), pltpu.VMEM((NS, EARLY, NP, 128), F32), pltpu.VMEM((EARLY, NS, NP, 128), F32),
            pltpu.VMEM((NC + EARLY, 2, 128, 128), F32),
            pltpu.VMEM((NS, NE, NP, 128), F32), pltpu.VMEM((NE, NS, NP, 128), F32), pltpu.VMEM((2, 128, 128), F32),
            pltpu.VMEM((NF, 2, 128, 128), BF16), pltpu.VMEM((NF, 2, 128, 128), BF16),
            pltpu.VMEM((NE, 2, NF, NP, 128), BF16),
            pltpu.VMEM((LIVE + 1, 128, 128), BF16), pltpu.VMEM((NG, 128, 128), BF16), pltpu.VMEM((NG, 128, 128), BF16),
            dma((5,)), dma(()), dma(()), dma((7,)), dma((7,)), dma(()), dma((EARLY,)),
            dma(()), dma((NE,)), dma(()), dma((NE,)), dma(()), dma(()), dma(()),
        ],
        compiler_params=pltpu.CompilerParams(
            collective_id=0, has_side_effects=True, vmem_limit_bytes=62 * 1024 * 1024
        ),
        name="beam_migration",
    )(tab, traces, send, win, jnp.asarray(t0), jnp.asarray(t1), depth, lat, spr)


def body(mesh, traces, send_table, window_slots, ray_depth, ray_lateral, ray_spread, ray_index, foot_count, foot_tiles, tile_owner):
    tab = prep(foot_count, ray_index, foot_tiles, tile_owner)
    return fused(mesh, tab, traces[0], send_table[0], window_slots[0], ray_depth[0], ray_lateral, ray_spread)


def solution(mesh):
    in_specs = (
        P("shot", "beam", None),
        P("shot", None, None, None),
        P("shot", "beam", None),
        P("shot", "beam", None, None),
        P("beam", None, None),
        P("beam", None, None),
        P("beam", None),
        P("beam", None),
        P(),
        P(),
    )
    return jax.shard_map(functools.partial(body, mesh), mesh=mesh, in_specs=in_specs, out_specs=P(("shot", "beam"), None, None), check_vma=False)
```

```python
import functools
import math

import jax
import jax.numpy as jnp
import numpy as np
from jax import lax
from jax.experimental import pallas as pl
from jax.experimental.pallas import tpu as pltpu
from jax.sharding import PartitionSpec as P

MESH = pl.DeviceIdType.MESH
F32, BF16 = jnp.float32, jnp.bfloat16
NF, NP, NC, WIN, FOOT, LIVE = 64, 32, 8, 32, 12, 80
NS, NG, NE = 8, 16, 10
W0, DW, MID = 4.0, 60.0 / 64, 32
TWO_PI = 2.0 * math.pi
KP = 16
EARLY = 2
AT_ROW, AT_CEN, AT_PICK, AT_SLOT = 0, 1, 2, 3


def fit():
    x = np.cos(np.pi * (np.arange(400) + 0.5) / 400)
    q = (x * 0.5 + 0.5) * 0.25
    a = 2 * np.pi * np.sqrt(q)

    def poly(y, deg):
        c = np.polynomial.chebyshev.Chebyshev.fit(q, y, deg, domain=[0, 0.25])
        return [float(v) for v in c.convert(kind=np.polynomial.Polynomial).coef]

    return poly(np.cos(a), 7), poly(np.sin(a) / np.sqrt(q), 6)


COS_C, SIN_C = fit()


def sincos_turns(t):
    r = t - jnp.round(t)
    q = r * r
    cs = COS_C[-1]
    for c in COS_C[-2::-1]:
        cs = cs * q + c
    sn = SIN_C[-1]
    for c in SIN_C[-2::-1]:
        sn = sn * q + c
    return cs, sn * r


def stack_tables():
    f32 = np.float32
    angular = (2.0 * math.pi * (4.0 + 60.0 * np.arange(NF, dtype=f32) / NF)).astype(f32)
    centred = np.arange(WIN, dtype=f32) - f32(0.5 * (WIN - 1))
    taper = (np.exp(-((centred / f32(8.0)) ** 2)) / f32(math.sqrt(WIN))).astype(f32)
    slow = (f32(2e-05) * (np.arange(NP, dtype=f32) - f32(15.5))).astype(f32)
    angle = (angular[None, None, :] * slow[None, :, None]) * (f32(25.0) * centred)[:, None, None]
    sr = (taper[:, None, None] * np.cos(angle)).astype(BF16)
    si = (-taper[:, None, None] * np.sin(angle)).astype(BF16)
    return np.concatenate([sr, sr], 2), np.concatenate([-si, si], 2)


def lateral(tl, sp, l_scr, e):
    lc, ls = sincos_turns(W0 * tl)
    dm = jnp.exp(sp * (-TWO_PI * W0))
    lr, li = lc * dm, -(ls * dm)
    uc, us = sincos_turns(DW * tl)
    du = jnp.exp(sp * (-TWO_PI * DW))
    ur, ui = uc * du, -(us * du)
    for f in range(NF):
        l_scr[e, 0, f] = lr.astype(BF16)
        l_scr[e, 1, f] = li.astype(BF16)
        if f < NF - 1:
            lr, li = lr * ur - li * ui, lr * ui + li * ur


def depth_unit(c, d_scr, i, tdt, bt):
    z = pl.ds(pl.multiple_of(i * 16, 16), 16)
    seeds = []
    for h in range(2):
        t = tdt[h, z, :]
        c1, s1 = sincos_turns((W0 + DW * MID) * t)
        uc, us = sincos_turns(DW * t)
        c0, s0 = c1 * uc + s1 * us, s1 * uc - c1 * us
        seeds.append((c0 + s0, s0 - c0, c1 + s1, s1 - c1, uc + uc))

    def emit(f, st):
        mid = re = im = None
        for h in range(2):
            br = bt[c, h, f : f + 1, :]
            bi = bt[c, h, NF + f : NF + f + 1, :]
            bm = bt[c, h, 2 * NF + f : 2 * NF + f + 1, :]
            plus, minus = st[h][2], st[h][3]
            k = (plus - minus) * bm
            mid = k if mid is None else mid + k
            re = bi * plus if re is None else re + bi * plus
            im = br * minus if im is None else im + br * minus
        d_scr[f, 0, z, :] = (mid - re).astype(BF16)
        d_scr[f, 1, z, :] = (mid + im).astype(BF16)

    def step(st):
        return [(x[2], x[3], s[4] * x[2] - x[0], s[4] * x[3] - x[1]) for x, s in zip(st, seeds)]

    st = [s[:4] for s in seeds]
    for f in range(MID, NF):
        emit(f, st)
        if f < NF - 1:
            st = step(st)
    st = [(s[2], s[3], s[0], s[1]) for s in seeds]
    for f in range(MID - 1, -1, -1):
        emit(f, st)
        if f > 0:
            st = step(st)


def mm_piece(e, d_scr, i, l_scr, accs):
    part = i % 2
    f0 = (i // 2) * KP
    blank = jnp.zeros((256, 128), BF16)
    for t in range(KP // 2):
        unit = t % 2
        f = f0 + 2 * t
        la, lb = l_scr[e, part, f], l_scr[e, part, f + 1]
        rhs = jnp.concatenate([jnp.concatenate([la] * 4 + [lb] * 4, 0), blank], 1)
        stage = (t // 2) % 2
        pltpu.matmul_push_rhs(rhs, stage, unit)
        lhs = jnp.concatenate([d_scr[f, part], d_scr[f + 1, part]], 1)
        pltpu.matmul_acc_lhs(accs[unit], lhs, load_staged_rhs=stage)


def mm_result(accs):
    return pltpu.matmul_pop(accs[0])[:, :128] + pltpu.matmul_pop(accs[1])[:, :128]


def row_to_col(row):
    return jnp.broadcast_to(row, (128, 128)).T


def prep_kernel(count, index, foot, foot_v, owner_v, out_ref):
    shot = lax.axis_index("shot")
    beam = lax.axis_index("beam")
    n = lax.broadcasted_iota(jnp.int32, (1, 128), 1)
    cen = jnp.zeros((1, 128), jnp.int32)
    base = jnp.zeros((1, 128), jnp.int32)
    total = jnp.int32(0)
    for c in range(NC):
        prior = total
        total = total + count[0, c]
        cen = cen + jnp.where(n >= total, 1, 0)
        base = jnp.where(n >= prior, prior, base)
    eid = cen * FOOT + n - base
    rows = jnp.zeros((1, 128), jnp.int32)
    tile = jnp.zeros((1, 128), jnp.int32)
    for c in range(NC):
        for k in range(FOOT):
            hit = eid == c * FOOT + k
            rows = jnp.where(hit, index[c, k], rows)
            tile = jnp.where(hit, foot[k, beam * NC + c], tile)
    live = n < LIVE
    down = lax.broadcasted_iota(jnp.int32, (128, 128), 0).astype(F32)
    across = lax.broadcasted_iota(jnp.int32, (128, 128), 1).astype(F32)
    tile = tile.astype(F32)
    owners = owner_v[...].astype(F32)
    owner = jnp.zeros((1, 128), F32)
    for q in range(OWN_ROWS):
        hit = down + 128.0 * q == tile
        owner = owner + jnp.sum(jnp.where(hit, row_to_col(owners[q : q + 1]), 0.0), axis=0, keepdims=True)
    owner = jnp.where(live, owner, -1.0)
    same = (row_to_col(owner) == owner) & (down < across)
    rank = jnp.sum(jnp.where(same, 1.0, 0.0), axis=0, keepdims=True)
    key = jnp.where(live, (owner - (shot * NG).astype(F32)) * NC + rank, -1.0)
    hit = row_to_col(key) == across
    picks = LIVE + jnp.sum(jnp.where(hit, down - LIVE, 0.0), axis=0, keepdims=True)
    me = (shot * NG + beam).astype(F32)
    number = (
        lax.broadcasted_iota(jnp.int32, (OWN_ROWS, 128), 0) * 128 + lax.broadcasted_iota(jnp.int32, (OWN_ROWS, 128), 1)
    ).astype(F32)
    held = owners == me
    named = foot_v[...].astype(F32)
    slot = jnp.zeros(named.shape, F32)
    at = jnp.full((1, 1), -1.0, F32)
    for i in range(4):
        left = jnp.where(held & (number > at), number, 1e6)
        at = jnp.min(jnp.min(left, axis=0, keepdims=True), axis=1, keepdims=True)
        slot = jnp.where(named == at, float(i), slot)
    slot = jnp.max(slot, axis=0, keepdims=True)
    out_ref[...] = jnp.zeros((8, 128), jnp.int32)
    out_ref[AT_ROW : AT_ROW + 1] = rows
    out_ref[AT_CEN : AT_CEN + 1] = jnp.minimum(cen, NC - 1)
    out_ref[AT_PICK : AT_PICK + 1] = picks.astype(jnp.int32)
    out_ref[AT_SLOT : AT_SLOT + 1] = slot.astype(jnp.int32)


OWN_ROWS = NS * NG * 4 // 128


def prep(foot_count, ray_index, foot_tiles, tile_owner):
    vm, sm = pl.BlockSpec(memory_space=pltpu.VMEM), pl.BlockSpec(memory_space=pltpu.SMEM)
    return pl.pallas_call(
        prep_kernel,
        out_shape=jax.ShapeDtypeStruct((8, 128), jnp.int32),
        in_specs=[sm, sm, sm, vm, vm],
        out_specs=vm,
        name="entry_table",
    )(foot_count, ray_index, foot_tiles.T, foot_tiles.T, tile_owner.reshape(OWN_ROWS, 128))


def one_hot(x, count, width):
    xt = jnp.concatenate([x.astype(F32), jnp.zeros((x.shape[0], 128 - count), F32)], 1).T
    lanes = lax.broadcasted_iota(jnp.int32, (count, width), 1).astype(F32)
    parts = [jnp.where(lanes == xt[:count, r : r + 1], 1.0, 0.0) for r in range(x.shape[0])]
    return jnp.concatenate(parts, 0).astype(BF16)


def kernel(
    mesh, tab, traces, send_ref, win_ref, t0_hbm, t1_hbm, depth_hbm, lat_hbm, spr_hbm, out_ref,
    t0, t1, depth_v, lat_v, spr_v, tr_out, tr_in, win_s, win_r, ball, b_own, b_out, b_in, bt, td_out, td_in, tdt,
    d0, d1, l_scr, tiles, dense, got,
    tab_sem, trs, trr, bs, br_sem, bes, ber, tds, tdr, tls, tln, tlr, ows, owr,
):
    shot = lax.axis_index("shot")
    beam = lax.axis_index("beam")
    way = 1 - 2 * lax.rem(shot, 2)
    partner = shot + way
    ahead = lax.rem(shot + 2 * way + NS, NS)
    behind = lax.rem(shot - 2 * way + NS, NS)
    ring = (
        (shot, ahead), (shot, behind), (shot, partner),
        (behind, ahead), (behind, ahead + way), (behind, partner), (ahead, partner),
    )

    def at_shot(s):
        return dict(device_id={"shot": s, "beam": beam}, device_id_type=MESH)

    def at_beam(g):
        return dict(device_id={"shot": shot, "beam": g}, device_id_type=MESH)

    def await_all(ref, sem):
        pltpu.make_async_copy(ref, ref, sem).wait()

    barrier = pltpu.get_barrier_semaphore()
    for d in range(1, NG):
        pl.semaphore_signal(barrier, inc=1, **at_beam(lax.rem(beam + d, NG)))
    for d in range(1, NS):
        pl.semaphore_signal(barrier, inc=1, **at_shot(lax.rem(shot + d, NS)))
    pairs = ((depth_hbm, depth_v), (lat_hbm, lat_v), (spr_hbm, spr_v), (t0_hbm, t0), (t1_hbm, t1))
    loads = [pltpu.make_async_copy(h, v, tab_sem.at[n]) for n, (h, v) in enumerate(pairs)]
    for cp in loads:
        cp.start()

    def select(pick, rows):
        def go(total):
            wide = jnp.concatenate([rows, jnp.zeros((256, 128), BF16)], 1)
            pltpu.matmul_push_rhs(wide, 0, 0)
            pltpu.matmul_acc_lhs(total, pick, load_staged_rhs=0)
            return pltpu.matmul_pop(total)[:, :128]

        with jax.sharding.use_abstract_mesh(mesh.abstract_mesh):
            kind = pltpu.ACC(0)((256, 256), F32)
        return pl.run_scoped(go, kind)

    pick = one_hot(send_ref[beam], 16, 256)
    chosen = select(pick, traces[...]).astype(BF16)
    tr_out[...] = chosen.reshape(NG, 16, 128)
    tr_in[beam] = tr_out[beam]
    pl.semaphore_wait(barrier, NS - 1 + NG - 1)

    def trace_copy(d):
        g = lax.rem(beam + d, NG)
        return pltpu.make_async_remote_copy(
            src_ref=tr_out.at[g], dst_ref=tr_in.at[beam], send_sem=trs, recv_sem=trr, **at_beam(g)
        )

    for d in range(1, NG):
        trace_copy(d).start()

    loads[0].wait()

    def gather(e, _):
        for j in range(NS):
            td_out[j, e] = depth_v[tab[AT_ROW, j * NE + e]]
        td_in[e, shot] = depth_v[tab[AT_ROW, shot * NE + e]]
        return 0

    lax.fori_loop(0, NE, gather, 0)

    def depth_copy(e, d):
        j = lax.rem(shot + d, NS)
        return pltpu.make_async_remote_copy(
            src_ref=td_out.at[j, e], dst_ref=td_in.at[e, shot], send_sem=tds, recv_sem=tdr.at[e], **at_shot(j)
        )

    for d in range(1, NS):
        depth_copy(0, d).start()
    loads[1].wait()
    loads[2].wait()

    def lat(e, _):
        r = tab[AT_ROW, shot * NE + e]
        lateral(lat_v[r], spr_v[r], l_scr, e)
        return 0

    lax.fori_loop(0, NE // 2, lat, 0)
    pick = one_hot(win_ref[...], WIN, NG * 16)
    loads[3].wait()
    loads[4].wait()

    await_all(tr_in.at[0 : NG - 1], trr)
    win = select(pick, tr_in[...].reshape(NG * 16, 128))
    win_s[...] = win.reshape(NC, WIN, 128)
    win_r[...] = pltpu.roll(win, 64, 1).reshape(NC, WIN, 128)

    def stack(c, _):
        a = jnp.zeros((NP, 128), F32)
        for k in range(WIN):
            a = a + (t0[k].astype(F32) * win_s[c, k : k + 1, :] + t1[k].astype(F32) * win_r[c, k : k + 1, :])
        b_own[c] = a * (1.0 / math.sqrt(NP * NF))
        return 0

    lax.fori_loop(0, NC, stack, 0)

    def early_copy(e, d):
        j = lax.rem(shot + d, NS)
        return pltpu.make_async_remote_copy(
            src_ref=b_out.at[j, e], dst_ref=b_in.at[e, shot], send_sem=bes, recv_sem=ber.at[e], **at_shot(j)
        )

    for e in range(EARLY):
        for j in range(NS):
            b_out[j, e] = b_own[tab[AT_CEN, j * NE + e]]
        b_in[e, shot] = b_own[tab[AT_CEN, shot * NE + e]]

    def beam_copy(n):
        item, to = ring[n]
        return pltpu.make_async_remote_copy(
            src_ref=b_own if n < 3 else ball.at[item], dst_ref=ball.at[item],
            send_sem=bs.at[n], recv_sem=br_sem.at[n], **at_shot(to),
        )

    def tile_copy(e, n):
        item, to = ring[n]
        return pltpu.make_async_remote_copy(
            src_ref=tiles.at[item * NE + e], dst_ref=tiles.at[item * NE + e],
            send_sem=tls, recv_sem=tln.at[e] if n < 2 else tlr, **at_shot(to),
        )

    def relay(e):
        await_all(tiles.at[0:2], tln.at[e])
        for n in range(3, 7):
            tile_copy(e, n).start()

    def early_send(e):
        for d in range(1, NS):
            early_copy(e, d).start()

    def depth_send(e):
        for d in range(1, NS):
            depth_copy(e, d).start()

    early_send(0)
    for n in range(3):
        beam_copy(n).start()
    depth_send(1)
    for e in range(1, EARLY):
        early_send(e)
    ball[shot] = b_own[...]
    lax.fori_loop(NE // 2, NE, lat, 0)

    def share(e, accs):
        tiles[shot * NE + e] = mm_result(accs).astype(BF16)
        for n in range(3):
            tile_copy(e, n).start()

    def both(accs, e, c, dst, src, after=None):
        await_all(td_in.at[e, 0 : NS - 1], tdr.at[e])
        for h in range(2):
            tdt[h] = td_in[e, 4 * h : 4 * h + 4].reshape(128, 128).T

        def unit(i, _):
            if src is not None:
                mm_piece(e - 1, src, i, l_scr, accs)
            depth_unit(c, dst, i, tdt, bt)
            return 0

        lax.fori_loop(0, 8, unit, 0)
        if src is not None:
            share(e - 1, accs)
        if after is not None:
            after()
        if isinstance(e, int):
            depth_send(e + 2)
        else:
            relay(e - 2)

            @pl.when(e + 2 < NE)
            def _():
                depth_send(e + 2)

    def put_beams(c, h, v):
        bt[c, h, 0 : 2 * NF] = v
        bt[c, h, 2 * NF : 3 * NF] = 0.5 * (v[:NF] + v[NF:])

    def early(e):
        await_all(b_in.at[e, 0 : NS - 1], ber.at[e])
        for h in range(2):
            put_beams(NC + e, h, b_in[e, 4 * h : 4 * h + 4].reshape(128, 128).T)

    def pass_beams():
        for n in range(2):
            beam_copy(n).wait_recv()
        for n in range(3, 7):
            beam_copy(n).start()

    def migrate(*accs):
        early(0)
        both(accs, 0, NC, d0, None, pass_beams)
        early(1)
        both(accs, 1, NC + 1, d1, d0)
        for n in range(2, 7):
            beam_copy(n).wait_recv()

        def turn(c, _):
            for h in range(2):
                put_beams(c, h, jnp.concatenate([ball[4 * h + s, c] for s in range(4)], 0).T)
            return 0

        lax.fori_loop(0, NC, turn, 0)

        def pair(k, _):
            both(accs, 2 * k, tab[AT_CEN, shot * NE + 2 * k], d0, d1)
            both(accs, 2 * k + 1, tab[AT_CEN, shot * NE + 2 * k + 1], d1, d0)
            return 0

        lax.fori_loop(1, NE // 2, pair, 0)

        def last(i, _):
            mm_piece(NE - 1, d1, i, l_scr, accs)
            return 0

        lax.fori_loop(0, 8, last, 0)
        share(NE - 1, accs)

    with jax.sharding.use_abstract_mesh(mesh.abstract_mesh):
        kinds = [pltpu.ACC(u)((128, 256), F32) for u in range(2)]
    pl.run_scoped(migrate, *kinds)
    relay(NE - 2)
    tiles[LIVE] = jnp.zeros((128, 128), BF16)
    relay(NE - 1)

    await_all(tiles.at[0 : 5 * NE], tlr)

    def owner_copy(d):
        g = lax.rem(beam + d, NG)
        return pltpu.make_async_remote_copy(
            src_ref=dense.at[g], dst_ref=got.at[beam], send_sem=ows, recv_sem=owr, **at_beam(g)
        )

    def gather_owner(d, _):
        g = lax.rem(beam + d, NG)
        s = tiles[tab[AT_PICK, g * NC]].astype(F32)
        for m in range(1, NC):
            s = s + tiles[tab[AT_PICK, g * NC + m]].astype(F32)
        dense[g] = s.astype(BF16)
        owner_copy(d).start()
        return 0

    lax.fori_loop(1, NG, gather_owner, 0)
    s = tiles[tab[AT_PICK, beam * NC]].astype(F32)
    for m in range(1, NC):
        s = s + tiles[tab[AT_PICK, beam * NC + m]].astype(F32)
    got[beam] = s.astype(BF16)

    await_all(tr_out.at[0 : NG - 1], trs)
    for n in range(7):
        beam_copy(n).wait_send()

    await_all(td_out.at[0 : NS - 1], tds)
    await_all(tiles.at[0 : LIVE - NE], tls)
    await_all(b_out.at[0 : NS - 1], bes)
    await_all(got.at[0 : NG - 1], owr)

    weights = []
    for g in range(NG):
        at = tab[AT_SLOT, g * NC]
        for c in range(1, NC):
            at = jnp.maximum(at, tab[AT_SLOT, g * NC + c])
        weights.append([jnp.where(at == slot, 1.0, 0.0) for slot in range(4)])

    def place(i, _):
        z = pl.ds(pl.multiple_of(i * 16, 16), 16)
        sums = [jnp.zeros((16, 128), F32)] * 4
        for g in range(NG):
            v = got[g, z, :].astype(F32)
            sums = [a + v * w for a, w in zip(sums, weights[g])]
        for slot in range(4):
            out_ref[slot, z, :] = sums[slot]
        return 0

    lax.fori_loop(0, 8, place, 0)
    await_all(dense.at[0 : NG - 1], ows)


def fused(mesh, tab, traces, send, win, depth, lat, spr):
    t0, t1 = stack_tables()
    vm = pl.BlockSpec(memory_space=pltpu.VMEM)
    hbm = pl.BlockSpec(memory_space=pl.ANY)
    dma = pltpu.SemaphoreType.DMA
    return pl.pallas_call(
        functools.partial(kernel, mesh),
        out_shape=jax.ShapeDtypeStruct((4, 128, 128), F32),
        in_specs=[pl.BlockSpec(memory_space=pltpu.SMEM), vm, vm, vm, hbm, hbm, hbm, hbm, hbm],
        out_specs=vm,
        scratch_shapes=[
            pltpu.VMEM((WIN, NP, 128), BF16), pltpu.VMEM((WIN, NP, 128), BF16),
            pltpu.VMEM((256, 32, 128), F32), pltpu.VMEM((256, 32, 128), F32), pltpu.VMEM((256, 32, 128), F32),
            pltpu.VMEM((NG, 16, 128), BF16), pltpu.VMEM((NG, 16, 128), BF16),
            pltpu.VMEM((NC, WIN, 128), F32), pltpu.VMEM((NC, WIN, 128), F32),
            pltpu.VMEM((NS, NC, NP, 128), F32), pltpu.VMEM((NC, NP, 128), F32), pltpu.VMEM((NS, EARLY, NP, 128), F32), pltpu.VMEM((EARLY, NS, NP, 128), F32),
            pltpu.VMEM((NC + EARLY, 2, 192, 128), F32),
            pltpu.VMEM((NS, NE, NP, 128), F32), pltpu.VMEM((NE, NS, NP, 128), F32), pltpu.VMEM((2, 128, 128), F32),
            pltpu.VMEM((NF, 2, 128, 128), BF16), pltpu.VMEM((NF, 2, 128, 128), BF16),
            pltpu.VMEM((NE, 2, NF, NP, 128), BF16),
            pltpu.VMEM((LIVE + 1, 128, 128), BF16), pltpu.VMEM((NG, 128, 128), BF16), pltpu.VMEM((NG, 128, 128), BF16),
            dma((5,)), dma(()), dma(()), dma((7,)), dma((7,)), dma(()), dma((EARLY,)),
            dma(()), dma((NE,)), dma(()), dma((NE,)), dma(()), dma(()), dma(()),
        ],
        compiler_params=pltpu.CompilerParams(
            collective_id=0, has_side_effects=True, vmem_limit_bytes=62 * 1024 * 1024
        ),
        name="beam_migration",
    )(tab, traces, send, win, jnp.asarray(t0), jnp.asarray(t1), depth, lat, spr)


def body(mesh, traces, send_table, window_slots, ray_depth, ray_lateral, ray_spread, ray_index, foot_count, foot_tiles, tile_owner):
    tab = prep(foot_count, ray_index, foot_tiles, tile_owner)
    return fused(mesh, tab, traces[0], send_table[0], window_slots[0], ray_depth[0], ray_lateral, ray_spread)


def solution(mesh):
    in_specs = (
        P("shot", "beam", None),
        P("shot", None, None, None),
        P("shot", "beam", None),
        P("shot", "beam", None, None),
        P("beam", None, None),
        P("beam", None, None),
        P("beam", None),
        P("beam", None),
        P(),
        P(),
    )
    return jax.shard_map(functools.partial(body, mesh), mesh=mesh, in_specs=in_specs, out_specs=P(("shot", "beam"), None, None), check_vma=False)
```

```python
import functools
import math

import jax
import jax.numpy as jnp
import numpy as np
from jax import lax
from jax.experimental import pallas as pl
from jax.experimental.pallas import tpu as pltpu
from jax.sharding import PartitionSpec as P

MESH = pl.DeviceIdType.MESH
F32, BF16 = jnp.float32, jnp.bfloat16
NF, NP, NC, WIN, FOOT, LIVE = 64, 32, 8, 32, 12, 80
NS, NG, NE = 8, 16, 10
W0, DW, MID = 4.0, 60.0 / 64, 32
TWO_PI = 2.0 * math.pi
KP = 16
EARLY = 2
AT_ROW, AT_CEN, AT_PICK, AT_SLOT = 0, 1, 2, 3


def fit():
    x = np.cos(np.pi * (np.arange(400) + 0.5) / 400)
    q = (x * 0.5 + 0.5) * 0.25
    a = 2 * np.pi * np.sqrt(q)

    def poly(y, deg):
        c = np.polynomial.chebyshev.Chebyshev.fit(q, y, deg, domain=[0, 0.25])
        return [float(v) for v in c.convert(kind=np.polynomial.Polynomial).coef]

    return poly(np.cos(a), 7), poly(np.sin(a) / np.sqrt(q), 6)


COS_C, SIN_C = fit()


def sincos_turns(t):
    r = t - jnp.round(t)
    q = r * r
    cs = COS_C[-1]
    for c in COS_C[-2::-1]:
        cs = cs * q + c
    sn = SIN_C[-1]
    for c in SIN_C[-2::-1]:
        sn = sn * q + c
    return cs, sn * r


def stack_tables():
    f32 = np.float32
    angular = (2.0 * math.pi * (4.0 + 60.0 * np.arange(NF, dtype=f32) / NF)).astype(f32)
    centred = np.arange(WIN, dtype=f32) - f32(0.5 * (WIN - 1))
    taper = (np.exp(-((centred / f32(8.0)) ** 2)) / f32(math.sqrt(WIN))).astype(f32)
    slow = (f32(2e-05) * (np.arange(NP, dtype=f32) - f32(15.5))).astype(f32)
    angle = (angular[None, None, :] * slow[None, :, None]) * (f32(25.0) * centred)[:, None, None]
    sr = (taper[:, None, None] * np.cos(angle)).astype(BF16)
    si = (-taper[:, None, None] * np.sin(angle)).astype(BF16)
    return np.concatenate([sr, sr], 2), np.concatenate([-si, si], 2)


def lateral(tl, sp, l_scr, e):
    lc, ls = sincos_turns(W0 * tl)
    dm = jnp.exp(sp * (-TWO_PI * W0))
    lr, li = lc * dm, -(ls * dm)
    uc, us = sincos_turns(DW * tl)
    du = jnp.exp(sp * (-TWO_PI * DW))
    ur, ui = uc * du, -(us * du)
    for f in range(NF):
        l_scr[e, 0, f] = lr.astype(BF16)
        l_scr[e, 1, f] = li.astype(BF16)
        if f < NF - 1:
            lr, li = lr * ur - li * ui, lr * ui + li * ur


def depth_unit(c, d_scr, i, tdt, bt):
    z = pl.ds(pl.multiple_of(i * 16, 16), 16)
    seeds = []
    for h in range(2):
        t = tdt[h, z, :]
        c1, s1 = sincos_turns((W0 + DW * MID) * t)
        uc, us = sincos_turns(DW * t)
        c0, s0 = c1 * uc + s1 * us, s1 * uc - c1 * us
        seeds.append((c0 + s0, s0 - c0, c1 + s1, s1 - c1, uc + uc))

    def emit(f, st):
        mid = re = im = None
        for h in range(2):
            br = bt[c, h, f : f + 1, :]
            bi = bt[c, h, NF + f : NF + f + 1, :]
            bm = bt[c, h, 2 * NF + f : 2 * NF + f + 1, :]
            plus, minus = st[h][2], st[h][3]
            k = (plus - minus) * bm
            mid = k if mid is None else mid + k
            re = bi * plus if re is None else re + bi * plus
            im = br * minus if im is None else im + br * minus
        d_scr[f, 0, z, :] = (mid - re).astype(BF16)
        d_scr[f, 1, z, :] = (mid + im).astype(BF16)

    def step(st):
        return [(x[2], x[3], s[4] * x[2] - x[0], s[4] * x[3] - x[1]) for x, s in zip(st, seeds)]

    st = [s[:4] for s in seeds]
    for f in range(MID, NF):
        emit(f, st)
        if f < NF - 1:
            st = step(st)
    st = [(s[2], s[3], s[0], s[1]) for s in seeds]
    for f in range(MID - 1, -1, -1):
        emit(f, st)
        if f > 0:
            st = step(st)


def mm_piece(e, d_scr, i, l_scr, accs):
    part = i % 2
    f0 = (i // 2) * KP
    blank = jnp.zeros((256, 128), BF16)
    for t in range(KP // 2):
        unit = t % 2
        f = f0 + 2 * t
        la, lb = l_scr[e, part, f], l_scr[e, part, f + 1]
        rhs = jnp.concatenate([jnp.concatenate([la] * 4 + [lb] * 4, 0), blank], 1)
        stage = (t // 2) % 2
        pltpu.matmul_push_rhs(rhs, stage, unit)
        lhs = jnp.concatenate([d_scr[f, part], d_scr[f + 1, part]], 1)
        pltpu.matmul_acc_lhs(accs[unit], lhs, load_staged_rhs=stage)


def mm_result(accs):
    return pltpu.matmul_pop(accs[0])[:, :128] + pltpu.matmul_pop(accs[1])[:, :128]


def row_to_col(row):
    return jnp.broadcast_to(row, (128, 128)).T


def prep_kernel(count, index, foot, foot_v, owner_v, out_ref):
    shot = lax.axis_index("shot")
    beam = lax.axis_index("beam")
    n = lax.broadcasted_iota(jnp.int32, (1, 128), 1)
    cen = jnp.zeros((1, 128), jnp.int32)
    base = jnp.zeros((1, 128), jnp.int32)
    total = jnp.int32(0)
    for c in range(NC):
        prior = total
        total = total + count[0, c]
        cen = cen + jnp.where(n >= total, 1, 0)
        base = jnp.where(n >= prior, prior, base)
    eid = cen * FOOT + n - base
    rows = jnp.zeros((1, 128), jnp.int32)
    tile = jnp.zeros((1, 128), jnp.int32)
    for c in range(NC):
        for k in range(FOOT):
            hit = eid == c * FOOT + k
            rows = jnp.where(hit, index[c, k], rows)
            tile = jnp.where(hit, foot[k, beam * NC + c], tile)
    live = n < LIVE
    down = lax.broadcasted_iota(jnp.int32, (128, 128), 0).astype(F32)
    across = lax.broadcasted_iota(jnp.int32, (128, 128), 1).astype(F32)
    tile = tile.astype(F32)
    owners = owner_v[...].astype(F32)
    owner = jnp.zeros((1, 128), F32)
    for q in range(OWN_ROWS):
        hit = down + 128.0 * q == tile
        owner = owner + jnp.sum(jnp.where(hit, row_to_col(owners[q : q + 1]), 0.0), axis=0, keepdims=True)
    owner = jnp.where(live, owner, -1.0)
    same = (row_to_col(owner) == owner) & (down < across)
    rank = jnp.sum(jnp.where(same, 1.0, 0.0), axis=0, keepdims=True)
    key = jnp.where(live, (owner - (shot * NG).astype(F32)) * NC + rank, -1.0)
    hit = row_to_col(key) == across
    picks = LIVE + jnp.sum(jnp.where(hit, down - LIVE, 0.0), axis=0, keepdims=True)
    me = (shot * NG + beam).astype(F32)
    number = (
        lax.broadcasted_iota(jnp.int32, (OWN_ROWS, 128), 0) * 128 + lax.broadcasted_iota(jnp.int32, (OWN_ROWS, 128), 1)
    ).astype(F32)
    held = owners == me
    named = foot_v[...].astype(F32)
    slot = jnp.zeros(named.shape, F32)
    at = jnp.full((1, 1), -1.0, F32)
    for i in range(4):
        left = jnp.where(held & (number > at), number, 1e6)
        at = jnp.min(jnp.min(left, axis=0, keepdims=True), axis=1, keepdims=True)
        slot = jnp.where(named == at, float(i), slot)
    slot = jnp.max(slot, axis=0, keepdims=True)
    out_ref[...] = jnp.zeros((8, 128), jnp.int32)
    out_ref[AT_ROW : AT_ROW + 1] = rows
    out_ref[AT_CEN : AT_CEN + 1] = jnp.minimum(cen, NC - 1)
    out_ref[AT_PICK : AT_PICK + 1] = picks.astype(jnp.int32)
    out_ref[AT_SLOT : AT_SLOT + 1] = slot.astype(jnp.int32)


OWN_ROWS = NS * NG * 4 // 128


def prep(foot_count, ray_index, foot_tiles, tile_owner):
    vm, sm = pl.BlockSpec(memory_space=pltpu.VMEM), pl.BlockSpec(memory_space=pltpu.SMEM)
    return pl.pallas_call(
        prep_kernel,
        out_shape=jax.ShapeDtypeStruct((8, 128), jnp.int32),
        in_specs=[sm, sm, sm, vm, vm],
        out_specs=vm,
        name="entry_table",
    )(foot_count, ray_index, foot_tiles.T, foot_tiles.T, tile_owner.reshape(OWN_ROWS, 128))


def one_hot(x, count, width):
    xt = jnp.concatenate([x.astype(F32), jnp.zeros((x.shape[0], 128 - count), F32)], 1).T
    lanes = lax.broadcasted_iota(jnp.int32, (count, width), 1).astype(F32)
    parts = [jnp.where(lanes == xt[:count, r : r + 1], 1.0, 0.0) for r in range(x.shape[0])]
    return jnp.concatenate(parts, 0).astype(BF16)


def kernel(
    mesh, tab, traces, send_ref, win_ref, t0_hbm, t1_hbm, depth_hbm, lat_hbm, spr_hbm, out_ref,
    t0, t1, depth_v, lat_v, spr_v, tr_out, tr_in, win_s, win_r, ball, b_own, b_out, b_in, bt, td_out, td_in, tdt,
    d0, d1, l_scr, tiles, dense, got,
    tab_sem, trs, trr, bs, br_sem, bes, ber, tds, tdr, tls, tln, tlr, ows, owr,
):
    shot = lax.axis_index("shot")
    beam = lax.axis_index("beam")
    way = 1 - 2 * lax.rem(shot, 2)
    partner = shot + way
    ahead = lax.rem(shot + 2 * way + NS, NS)
    behind = lax.rem(shot - 2 * way + NS, NS)
    ring = (
        (shot, ahead), (shot, behind), (shot, partner),
        (behind, ahead), (behind, ahead + way), (behind, partner), (ahead, partner),
    )

    def at_shot(s):
        return dict(device_id={"shot": s, "beam": beam}, device_id_type=MESH)

    def at_beam(g):
        return dict(device_id={"shot": shot, "beam": g}, device_id_type=MESH)

    def await_all(ref, sem):
        pltpu.make_async_copy(ref, ref, sem).wait()

    barrier = pltpu.get_barrier_semaphore()
    for d in range(1, NG):
        pl.semaphore_signal(barrier, inc=1, **at_beam(lax.rem(beam + d, NG)))
    for d in range(1, NS):
        pl.semaphore_signal(barrier, inc=1, **at_shot(lax.rem(shot + d, NS)))
    pairs = ((depth_hbm, depth_v), (lat_hbm, lat_v), (spr_hbm, spr_v), (t0_hbm, t0), (t1_hbm, t1))
    loads = [pltpu.make_async_copy(h, v, tab_sem.at[n]) for n, (h, v) in enumerate(pairs)]
    for cp in loads:
        cp.start()

    def select(pick, rows):
        def go(total):
            wide = jnp.concatenate([rows, jnp.zeros((256, 128), BF16)], 1)
            pltpu.matmul_push_rhs(wide, 0, 0)
            pltpu.matmul_acc_lhs(total, pick, load_staged_rhs=0)
            return pltpu.matmul_pop(total)[:, :128]

        with jax.sharding.use_abstract_mesh(mesh.abstract_mesh):
            kind = pltpu.ACC(0)((256, 256), F32)
        return pl.run_scoped(go, kind)

    pick = one_hot(send_ref[beam], 16, 256)
    chosen = select(pick, traces[...]).astype(BF16)
    tr_out[...] = chosen.reshape(NG, 16, 128)
    tr_in[beam] = tr_out[beam]
    pl.semaphore_wait(barrier, NS - 1 + NG - 1)

    def trace_copy(d):
        g = lax.rem(beam + d, NG)
        return pltpu.make_async_remote_copy(
            src_ref=tr_out.at[g], dst_ref=tr_in.at[beam], send_sem=trs, recv_sem=trr, **at_beam(g)
        )

    for d in range(1, NG):
        trace_copy(d).start()

    loads[0].wait()

    def gather(e, _):
        for j in range(NS):
            td_out[j, e] = depth_v[tab[AT_ROW, j * NE + e]]
        td_in[e, shot] = depth_v[tab[AT_ROW, shot * NE + e]]
        return 0

    lax.fori_loop(0, NE, gather, 0)

    def depth_copy(e, d):
        j = lax.rem(shot + d, NS)
        return pltpu.make_async_remote_copy(
            src_ref=td_out.at[j, e], dst_ref=td_in.at[e, shot], send_sem=tds, recv_sem=tdr.at[e], **at_shot(j)
        )

    for d in range(1, NS):
        depth_copy(0, d).start()
    loads[1].wait()
    loads[2].wait()

    def lat(e, _):
        r = tab[AT_ROW, shot * NE + e]
        lateral(lat_v[r], spr_v[r], l_scr, e)
        return 0

    lax.fori_loop(0, NE // 2, lat, 0)
    pick = one_hot(win_ref[...], WIN, NG * 16)
    loads[3].wait()
    loads[4].wait()

    await_all(tr_in.at[0 : NG - 1], trr)
    win = select(pick, tr_in[...].reshape(NG * 16, 128))
    win_s[...] = win.reshape(NC, WIN, 128)
    win_r[...] = pltpu.roll(win, 64, 1).reshape(NC, WIN, 128)

    def stack(c, _):
        a = jnp.zeros((NP, 128), F32)
        for k in range(WIN):
            a = a + (t0[k].astype(F32) * win_s[c, k : k + 1, :] + t1[k].astype(F32) * win_r[c, k : k + 1, :])
        b_own[c] = a * (1.0 / math.sqrt(NP * NF))
        return 0

    lax.fori_loop(0, NC, stack, 0)

    def early_copy(e, d):
        j = lax.rem(shot + d, NS)
        return pltpu.make_async_remote_copy(
            src_ref=b_out.at[j, e], dst_ref=b_in.at[e, shot], send_sem=bes, recv_sem=ber.at[e], **at_shot(j)
        )

    for e in range(EARLY):
        for j in range(NS):
            b_out[j, e] = b_own[tab[AT_CEN, j * NE + e]]
        b_in[e, shot] = b_own[tab[AT_CEN, shot * NE + e]]

    def beam_copy(n):
        item, to = ring[n]
        return pltpu.make_async_remote_copy(
            src_ref=b_own if n < 3 else ball.at[item], dst_ref=ball.at[item],
            send_sem=bs.at[n], recv_sem=br_sem.at[n], **at_shot(to),
        )

    def tile_copy(e, n):
        item, to = ring[n]
        return pltpu.make_async_remote_copy(
            src_ref=tiles.at[item * NE + e], dst_ref=tiles.at[item * NE + e],
            send_sem=tls, recv_sem=tln.at[e] if n < 2 else tlr, **at_shot(to),
        )

    def relay(e):
        await_all(tiles.at[0:2], tln.at[e])
        for n in range(3, 7):
            tile_copy(e, n).start()

    def early_send(e):
        for d in range(1, NS):
            early_copy(e, d).start()

    def depth_send(e):
        for d in range(1, NS):
            depth_copy(e, d).start()

    early_send(0)
    for n in range(3):
        beam_copy(n).start()
    depth_send(1)
    for e in range(1, EARLY):
        early_send(e)
    depth_send(2)
    ball[shot] = b_own[...]
    lax.fori_loop(NE // 2, NE, lat, 0)

    def share(e, accs):
        tiles[shot * NE + e] = mm_result(accs).astype(BF16)
        for n in range(3):
            tile_copy(e, n).start()

    def both(accs, e, c, dst, src, after=None):
        await_all(td_in.at[e, 0 : NS - 1], tdr.at[e])
        for h in range(2):
            tdt[h] = td_in[e, 4 * h : 4 * h + 4].reshape(128, 128).T

        def unit(i, _):
            if src is not None:
                mm_piece(e - 1, src, i, l_scr, accs)
            depth_unit(c, dst, i, tdt, bt)
            return 0

        lax.fori_loop(0, 8, unit, 0)
        if src is not None:
            share(e - 1, accs)
        if after is not None:
            after()
        if isinstance(e, int):
            depth_send(e + 3)
        else:
            relay(e - 2)

            @pl.when(e + 3 < NE)
            def _():
                depth_send(e + 3)

    def put_beams(c, h, v):
        bt[c, h, 0 : 2 * NF] = v
        bt[c, h, 2 * NF : 3 * NF] = 0.5 * (v[:NF] + v[NF:])

    def early(e):
        await_all(b_in.at[e, 0 : NS - 1], ber.at[e])
        for h in range(2):
            put_beams(NC + e, h, b_in[e, 4 * h : 4 * h + 4].reshape(128, 128).T)

    def pass_beams():
        for n in range(2):
            beam_copy(n).wait_recv()
        for n in range(3, 7):
            beam_copy(n).start()

    def migrate(*accs):
        early(0)
        both(accs, 0, NC, d0, None, pass_beams)
        early(1)
        both(accs, 1, NC + 1, d1, d0)
        for n in range(2, 7):
            beam_copy(n).wait_recv()

        def turn(c, _):
            for h in range(2):
                put_beams(c, h, jnp.concatenate([ball[4 * h + s, c] for s in range(4)], 0).T)
            return 0

        lax.fori_loop(0, NC, turn, 0)

        def pair(k, _):
            both(accs, 2 * k, tab[AT_CEN, shot * NE + 2 * k], d0, d1)
            both(accs, 2 * k + 1, tab[AT_CEN, shot * NE + 2 * k + 1], d1, d0)
            return 0

        lax.fori_loop(1, NE // 2, pair, 0)

        def last(i, _):
            mm_piece(NE - 1, d1, i, l_scr, accs)
            return 0

        lax.fori_loop(0, 8, last, 0)
        share(NE - 1, accs)

    with jax.sharding.use_abstract_mesh(mesh.abstract_mesh):
        kinds = [pltpu.ACC(u)((128, 256), F32) for u in range(2)]
    pl.run_scoped(migrate, *kinds)
    relay(NE - 2)
    tiles[LIVE] = jnp.zeros((128, 128), BF16)
    relay(NE - 1)

    await_all(tiles.at[0 : 5 * NE], tlr)

    def owner_copy(d):
        g = lax.rem(beam + d, NG)
        return pltpu.make_async_remote_copy(
            src_ref=dense.at[g], dst_ref=got.at[beam], send_sem=ows, recv_sem=owr, **at_beam(g)
        )

    def gather_owner(d, _):
        g = lax.rem(beam + d, NG)
        s = tiles[tab[AT_PICK, g * NC]].astype(F32)
        for m in range(1, NC):
            s = s + tiles[tab[AT_PICK, g * NC + m]].astype(F32)
        dense[g] = s.astype(BF16)
        owner_copy(d).start()
        return 0

    lax.fori_loop(1, NG, gather_owner, 0)
    s = tiles[tab[AT_PICK, beam * NC]].astype(F32)
    for m in range(1, NC):
        s = s + tiles[tab[AT_PICK, beam * NC + m]].astype(F32)
    got[beam] = s.astype(BF16)

    await_all(tr_out.at[0 : NG - 1], trs)
    for n in range(7):
        beam_copy(n).wait_send()

    await_all(td_out.at[0 : NS - 1], tds)
    await_all(tiles.at[0 : LIVE - NE], tls)
    await_all(b_out.at[0 : NS - 1], bes)
    await_all(got.at[0 : NG - 1], owr)

    weights = []
    for g in range(NG):
        at = tab[AT_SLOT, g * NC]
        for c in range(1, NC):
            at = jnp.maximum(at, tab[AT_SLOT, g * NC + c])
        weights.append([jnp.where(at == slot, 1.0, 0.0) for slot in range(4)])

    def place(i, _):
        z = pl.ds(pl.multiple_of(i * 16, 16), 16)
        sums = [jnp.zeros((16, 128), F32)] * 4
        for g in range(NG):
            v = got[g, z, :].astype(F32)
            sums = [a + v * w for a, w in zip(sums, weights[g])]
        for slot in range(4):
            out_ref[slot, z, :] = sums[slot]
        return 0

    lax.fori_loop(0, 8, place, 0)
    await_all(dense.at[0 : NG - 1], ows)


def fused(mesh, tab, traces, send, win, depth, lat, spr):
    t0, t1 = stack_tables()
    vm = pl.BlockSpec(memory_space=pltpu.VMEM)
    hbm = pl.BlockSpec(memory_space=pl.ANY)
    dma = pltpu.SemaphoreType.DMA
    return pl.pallas_call(
        functools.partial(kernel, mesh),
        out_shape=jax.ShapeDtypeStruct((4, 128, 128), F32),
        in_specs=[pl.BlockSpec(memory_space=pltpu.SMEM), vm, vm, vm, hbm, hbm, hbm, hbm, hbm],
        out_specs=vm,
        scratch_shapes=[
            pltpu.VMEM((WIN, NP, 128), BF16), pltpu.VMEM((WIN, NP, 128), BF16),
            pltpu.VMEM((256, 32, 128), F32), pltpu.VMEM((256, 32, 128), F32), pltpu.VMEM((256, 32, 128), F32),
            pltpu.VMEM((NG, 16, 128), BF16), pltpu.VMEM((NG, 16, 128), BF16),
            pltpu.VMEM((NC, WIN, 128), F32), pltpu.VMEM((NC, WIN, 128), F32),
            pltpu.VMEM((NS, NC, NP, 128), F32), pltpu.VMEM((NC, NP, 128), F32), pltpu.VMEM((NS, EARLY, NP, 128), F32), pltpu.VMEM((EARLY, NS, NP, 128), F32),
            pltpu.VMEM((NC + EARLY, 2, 192, 128), F32),
            pltpu.VMEM((NS, NE, NP, 128), F32), pltpu.VMEM((NE, NS, NP, 128), F32), pltpu.VMEM((2, 128, 128), F32),
            pltpu.VMEM((NF, 2, 128, 128), BF16), pltpu.VMEM((NF, 2, 128, 128), BF16),
            pltpu.VMEM((NE, 2, NF, NP, 128), BF16),
            pltpu.VMEM((LIVE + 1, 128, 128), BF16), pltpu.VMEM((NG, 128, 128), BF16), pltpu.VMEM((NG, 128, 128), BF16),
            dma((5,)), dma(()), dma(()), dma((7,)), dma((7,)), dma(()), dma((EARLY,)),
            dma(()), dma((NE,)), dma(()), dma((NE,)), dma(()), dma(()), dma(()),
        ],
        compiler_params=pltpu.CompilerParams(
            collective_id=0, has_side_effects=True, vmem_limit_bytes=62 * 1024 * 1024
        ),
        name="beam_migration",
    )(tab, traces, send, win, jnp.asarray(t0), jnp.asarray(t1), depth, lat, spr)


def body(mesh, traces, send_table, window_slots, ray_depth, ray_lateral, ray_spread, ray_index, foot_count, foot_tiles, tile_owner):
    tab = prep(foot_count, ray_index, foot_tiles, tile_owner)
    return fused(mesh, tab, traces[0], send_table[0], window_slots[0], ray_depth[0], ray_lateral, ray_spread)


def solution(mesh):
    in_specs = (
        P("shot", "beam", None),
        P("shot", None, None, None),
        P("shot", "beam", None),
        P("shot", "beam", None, None),
        P("beam", None, None),
        P("beam", None, None),
        P("beam", None),
        P("beam", None),
        P(),
        P(),
    )
    return jax.shard_map(functools.partial(body, mesh), mesh=mesh, in_specs=in_specs, out_specs=P(("shot", "beam"), None, None), check_vma=False)
```
